256 devices in a mesh: row: 8 (over y, x_hi), col: 32 (over z, x_lo, core).
Axes of the slice: x: 4 (x_hi: 2, x_lo: 2; x = x_hi * 2 + x_lo), y: 4, z: 8, core: 2. Of those that a mesh axis runs over, the one named last changes fastest.
Arguments:
- tokens: bfloat16 [256, 12288], P('col', 'row'), may hold values from -6 to 6
- cotangent: bfloat16 [256, 12288], P('col', 'row'), may hold values from -6 to 6
- w1_mask: int32 [96, 384], P('row', 'col'), may hold values from 0 to 1, as said below
- w1_blocks: bfloat16 [8, 32, 48, 128, 128], P('row', 'col'), may hold values from -0.109375 to 0.109375
- bias: bfloat16 [49152], P('col'), may hold values from -4 to 4
- w2_mask: int32 [384, 96], P('col', 'row'), may hold values from 0 to 1, as said below
- w2_blocks: bfloat16 [8, 32, 48, 128, 128], P('row', 'col'), may hold values from -0.0546875 to 0.0546875
Outputs:
- out: bfloat16 [256, 12288], P('col', 'row')
- tokens_grad: bfloat16 [256, 12288], P('col', 'row')
- w1_grad: float32 [8, 32, 48, 128, 128], P('row', 'col')
- w2_grad: float32 [8, 32, 48, 128, 128], P('row', 'col')
- bias_grad: float32 [49152], P('col')
The draws below stay inside these ranges and needn't reach their ends.
Inputs may be any that keep to these rules, and one draw needn't show every extreme that they name: `w1_mask`: in every block row, each aligned group of 8 blocks along the columns holds exactly two ones. One device's tile of 12 x 12 blocks holds at most 48 ones, and in every draw some device's tile holds exactly 48. `w2_mask`: in every block row, each aligned group of 8 blocks along the columns holds exactly two ones. One device's tile of 12 x 12 blocks holds at most 48 ones, and in every draw some device's tile holds exactly 48.
All inputs are finite; a program needn't handle non-finite values.
Results may differ from the reference program's by a relative error of at most 0.005.
Values may be sent and summed in bfloat16 or wider, within the bound.
A program may use at most 64 MiB of HBM per device.

```python
import math
import jax
import jax.numpy as jnp
from jax import lax

D = 12288
FF = 49152
BLK = 128
TOKENS = 256
TBR = 12
TBC = 12
CAP1 = 48
CAP2 = 48
N_ROW = 8
N_COL = 32


def pair_mask(key, row_count, col_count, tile_width, band_height):
    groups = col_count // 8
    splits = jax.random.split(key, 6)
    first_pos = jax.random.randint(splits[0], (row_count, groups), 0, 8)
    second_pos = (first_pos + jax.random.randint(splits[1], (row_count, groups), 1, 8)) % 8
    band_index = jax.random.randint(splits[2], (), 0, row_count // band_height)
    tile_index = jax.random.randint(splits[3], (), 0, col_count // tile_width)
    group_start = jnp.arange(groups) * 8
    low_edge = jnp.clip(tile_index * tile_width - group_start, 0, 8)
    high_edge = jnp.clip(tile_index * tile_width + tile_width - group_start, 0, 8)
    span_size = high_edge - low_edge
    offset_one = jax.random.randint(splits[4], (row_count, groups), 0, 1 << 20)
    offset_two = jax.random.randint(splits[5], (row_count, groups), 0, 1 << 20)
    safe_span = jnp.maximum(span_size, 2)[None, :]
    pick_one = offset_one % safe_span
    pick_two = (pick_one + 1 + offset_two % (safe_span - 1)) % safe_span
    inside = (jnp.arange(row_count)[:, None] // band_height == band_index) & (span_size[None, :] >= 2)
    first_pos = jnp.where(inside, low_edge[None, :] + pick_one, first_pos)
    second_pos = jnp.where(inside, low_edge[None, :] + pick_two, second_pos)
    places = jnp.arange(8)
    marks = (places == first_pos[..., None]) | (places == second_pos[..., None])
    return marks.reshape(row_count, col_count).astype(jnp.int32)


def draw_w1_mask(key, part):
    return pair_mask(jax.random.fold_in(key, 11), D // BLK, FF // BLK, TBC, TBR)


def draw_w2_mask(key, part):
    return pair_mask(jax.random.fold_in(key, 23), FF // BLK, D // BLK, TBR, TBC)


def block_levels(own_key, shape, cuts, least, top_value):
    gain, own = 1.0, jax.random.fold_in(own_key, 6)
    for dim, parts in cuts:
        steps = jnp.exp(jax.random.uniform(jax.random.fold_in(own, dim), (parts,), jnp.float32, least / len(cuts), top_value / len(cuts)))
        gain = gain * jnp.repeat(steps, shape[dim] // parts).reshape([-1 if axis == dim else 1 for axis in range(len(shape))])
    return gain


def centred(own_key, shape, deviation, reach, shards=(), held_as=jnp.bfloat16):
    result = jax.random.normal(own_key, shape, jnp.float32) * deviation
    if len(shards) > 0:
        result = block_levels(own_key, shape, shards, -0.22, 0.18) * result
    return jnp.clip(result, min=-reach, max=reach).astype(held_as)


def setup_inputs(seed: int = 0) -> dict:
    key_of = jax.random.split(jax.random.key(seed), 8)
    return {
        "tokens": centred(key_of[0], (TOKENS, D), 1.0, 6.0, ((0, 32), (1, 8))),
        "cotangent": centred(key_of[1], (TOKENS, D), 1.0, 6.0, ((0, 32), (1, 8))),
        "w1_mask": draw_w1_mask(jax.random.fold_in(key_of[7], 71), 0),
        "w1_blocks": centred(key_of[3], (N_ROW, N_COL, CAP1, BLK, BLK), (D // 4) ** -0.5, 0.109375, ((0, 8), (1, 32))),
        "bias": centred(key_of[4], (FF,), 1.0, 4.0, ((0, 32),)),
        "w2_mask": draw_w2_mask(jax.random.fold_in(key_of[7], 71), 0),
        "w2_blocks": centred(key_of[6], (N_ROW, N_COL, CAP2, BLK, BLK), (FF // 4) ** -0.5, 0.0546875, ((0, 8), (1, 32))),
    }


slope_const = math.sqrt(2.0 / math.pi)

def gelu_value(values):
    inner = slope_const * (values + 0.044715 * values * values * values)
    return 0.5 * values * (1.0 + jnp.tanh(inner))

def gelu_slope(values):
    inner = slope_const * (values + 0.044715 * values * values * values)
    tangent = jnp.tanh(inner)
    return 0.5 * (1.0 + tangent) + 0.5 * values * (1.0 - tangent * tangent) * slope_const * (1.0 + 3.0 * 0.044715 * values * values)

def slot_order(mask_tile, capacity):
    flat = mask_tile.reshape(-1)
    order = jnp.argsort(1 - flat, stable=True)[:capacity].astype(jnp.int32)
    live_slot = jnp.arange(capacity, dtype=jnp.int32) < jnp.sum(flat).astype(jnp.int32)
    return (order, live_slot)

def tile_dense(mask_tile, blocks):
    row_count, col_count = mask_tile.shape
    capacity = blocks.shape[0]
    block_width = blocks.shape[1]
    order, live_slot = slot_order(mask_tile, capacity)
    target = jnp.where(live_slot, order, row_count * col_count).astype(jnp.int32)
    dense = jnp.zeros((row_count * col_count + 1, block_width, block_width), blocks.dtype).at[target].set(blocks)
    dense = dense[:row_count * col_count]
    dense = dense.reshape(row_count, col_count, block_width, block_width).transpose(0, 2, 1, 3)
    return dense.reshape(row_count * block_width, col_count * block_width)

def tile_blocks(dense, mask_tile, capacity):
    row_count, col_count = mask_tile.shape
    block_width = dense.shape[0] // row_count
    pieces = dense.reshape(row_count, block_width, col_count, block_width).transpose(0, 2, 1, 3)
    pieces = pieces.reshape(row_count * col_count, block_width, block_width)
    order, live_slot = slot_order(mask_tile, capacity)
    return pieces[order] * live_slot[:, None, None].astype(jnp.float32)

def reference(tokens, cotangent, w1_mask, w1_blocks, bias, w2_mask, w2_blocks):
    hidden_width = TBC * BLK
    first_grid = w1_mask.reshape(N_ROW, TBR, N_COL, TBC)
    second_grid = w2_mask.reshape(N_COL, TBC, N_ROW, TBR)

    def column_step(running, column):
        out_acc, grad_acc = running
        first_masks = jnp.take(first_grid, column, axis=2)
        first_tiles = jnp.take(w1_blocks, column, axis=1)
        w1_column = jax.vmap(tile_dense)(first_masks, first_tiles).reshape(D, hidden_width)
        second_masks = jnp.take(second_grid, column, axis=0).transpose(1, 0, 2)
        second_tiles = jnp.take(w2_blocks, column, axis=1)
        w2_row = jax.vmap(tile_dense)(second_masks, second_tiles).transpose(1, 0, 2).reshape(hidden_width, D)
        bias_part = lax.dynamic_slice_in_dim(bias, column * hidden_width, hidden_width).astype(jnp.float32)
        hidden = jnp.dot(tokens, w1_column, preferred_element_type=jnp.float32) + bias_part
        activated = gelu_value(hidden).astype(jnp.bfloat16)
        out_acc = out_acc + jnp.dot(activated, w2_row, preferred_element_type=jnp.float32)
        grad_act = jnp.dot(cotangent, w2_row.T, preferred_element_type=jnp.float32)
        grad_hidden = (grad_act * gelu_slope(hidden)).astype(jnp.bfloat16)
        grad_acc = grad_acc + jnp.dot(grad_hidden, w1_column.T, preferred_element_type=jnp.float32)
        first_dense = jnp.dot(tokens.T, grad_hidden, preferred_element_type=jnp.float32).reshape(N_ROW, TBR * BLK, hidden_width)
        first_grad = jax.vmap(lambda dense, mask_tile: tile_blocks(dense, mask_tile, CAP1))(first_dense, first_masks)
        second_dense = jnp.dot(activated.T, cotangent, preferred_element_type=jnp.float32)
        second_dense = second_dense.reshape(hidden_width, N_ROW, TBR * BLK).transpose(1, 0, 2)
        second_grad = jax.vmap(lambda dense, mask_tile: tile_blocks(dense, mask_tile, CAP2))(second_dense, second_masks)
        bias_sum = lax.optimization_barrier(jnp.sum(grad_hidden.astype(jnp.float32), axis=0))
        return ((out_acc, grad_acc), (first_grad, second_grad, bias_sum))
    start = (jnp.zeros((TOKENS, D), jnp.float32), jnp.zeros((TOKENS, D), jnp.float32))
    (out_acc, grad_acc), (first_all, second_all, bias_all) = lax.scan(column_step, start, jnp.arange(N_COL, dtype=jnp.int32))
    w1_grad = first_all.transpose(1, 0, 2, 3, 4)
    w2_grad = second_all.transpose(1, 0, 2, 3, 4)
    return (out_acc.astype(jnp.bfloat16), grad_acc.astype(jnp.bfloat16), w1_grad, w2_grad, bias_all.reshape(-1))
```

```python
import functools
import math

import jax
import jax.numpy as jnp
from jax import lax
from jax.experimental import pallas as pl
from jax.experimental.pallas import tpu as pltpu
from jax.sharding import PartitionSpec as P

MESH = pl.DeviceIdType.MESH
BLK = 128
NCH = 3
F32 = jnp.float32
BF16 = jnp.bfloat16
SLOPE = math.sqrt(2.0 / math.pi)
Z_ORDER = (4, 3, 5, 2, 6, 1, 7)
Z_WAIT = (1, 7, 2, 6, 3, 5, 4)
ROW_ORDER = ((2, 1), (1, 1), (3, 1), (0, 1), (2, 0), (1, 0), (3, 0))


def dot_nn(a, b):
    return jnp.dot(a, b, preferred_element_type=F32)


def dot_nt(a, b):
    return lax.dot_general(a, b, (((1,), (1,)), ((), ())), preferred_element_type=F32)


def mega(
    tok, cot, m1, m2, bias, w1, w2,
    out_o, tg_o, t_o, c_o, a_o, g_o,
    t_all, c_all, a_all, g_all, w1d, w2d, wb1, wb2,
    h_send, ga_send, h_recv, ga_recv, slope_s,
    s_send, s_recv, own_a, b_send, b_recv, own_b, z_send, z_recv,
    loc, zs, zr, xs, xr, bs, br, rs_s, rs_r, ag_s, ag_r, la_s, la_r, lb_s, lb_r, lc_s, lc_r,
):
    rows = tok.shape[0]
    width = tok.shape[1]
    cw = width // NCH
    row, col = lax.axis_index("row"), lax.axis_index("col")
    y, xh = row // 2, row % 2
    z, xl, k = col // 4, (col // 2) % 2, col % 2

    def col_dev(zz, xx, kk):
        return (row, zz * 4 + xx * 2 + kk)

    def row_dev(dy, dx):
        return (((y + dy) % 4) * 2 + (xh + dx) % 2, col)

    def at_pos(zz, xx, kk):
        return kk * 16 + xx * 8 + zz

    def send(src, dst, ssem, rsem, dev):
        return pltpu.make_async_remote_copy(
            src_ref=src, dst_ref=dst, send_sem=ssem, recv_sem=rsem, device_id=dev, device_id_type=MESH
        )

    sib = col_dev(z, xl, 1 - k)
    xnb = col_dev(z, 1 - xl, k)
    peers = [row_dev(dy, dx) for dy, dx in ROW_ORDER]
    peers += [col_dev((z + d) % 8, xl, k) for d in range(1, 8)] + [sib, xnb]

    load1 = pltpu.make_async_copy(w1, wb1, loc.at[0])
    load2 = pltpu.make_async_copy(w2, wb2, loc.at[1])
    load1.start()
    load2.start()
    bar = pltpu.get_barrier_semaphore()
    for dev in peers:
        pl.semaphore_signal(bar, inc=1, device_id=dev, device_id_type=MESH)

    def densify(mask, blocks, dense):
        cap = blocks.shape[0]
        tr, tc = mask.shape

        def one_row(i, slot):
            for j in range(tc):
                live = mask[i, j]
                block = blocks[jnp.minimum(slot, cap - 1)]
                dense[pl.ds(pl.multiple_of(i * BLK, BLK), BLK), j * BLK:(j + 1) * BLK] = jnp.where(
                    live > 0, block, jnp.zeros_like(block)
                )
                slot = slot + live
            return slot

        lax.fori_loop(0, tr, one_row, jnp.int32(0))

    load1.wait()
    densify(m1, wb1, w1d)
    pl.semaphore_wait(bar, len(peers))

    pend = []

    ins, fulls = (tok, cot), (t_all, c_all)
    mine = at_pos(z, xl, k)
    zc, xc, bc, own = {}, {}, {}, {}
    for a in range(2):
        src, full = ins[a], fulls[a]
        for d in Z_ORDER:
            zc[a, d] = send(src, full.at[mine], zs.at[a, d], zr.at[a, d], col_dev((z + d) % 8, xl, k))
            zc[a, d].start()
        xc[a, 0] = send(src, full.at[mine], xs.at[a, 0], xr.at[a, 0], xnb)
        xc[a, 0].start()
        bc[a, 0] = send(src, full.at[mine], bs.at[a, 0], br.at[a, 0], sib)
        bc[a, 0].start()
        own[a] = pltpu.make_async_copy(src, full.at[mine], loc.at[2 + a])
        own[a].start()
    load2.wait()
    densify(m2, wb2, w2d)

    def forward_z(a):
        full = fulls[a]
        for d in Z_WAIT:
            zc[a, d].wait_recv()
            got = full.at[at_pos((z - d + 8) % 8, xl, k)]
            xc[a, d] = send(got, got, xs.at[a, d], xr.at[a, d], xnb)
            xc[a, d].start()
            bc[a, d] = send(got, got, bs.at[a, d], br.at[a, d], sib)
            bc[a, d].start()

    def forward_x(a):
        full = fulls[a]
        for d in (0,) + Z_WAIT:
            xc[a, d].wait_recv()
            got = full.at[at_pos((z - d + 8) % 8, 1 - xl, k)]
            bc[a, 8 + d] = send(got, got, bs.at[a, 8 + d], br.at[a, 8 + d], sib)
            bc[a, 8 + d].start()

    def finish(a):
        own[a].wait()
        for d in range(16):
            bc[a, d].wait_recv()

    def cols(n):
        return pl.ds(pl.multiple_of(n * cw, cw), cw)

    def share(dy, dx):
        return pl.ds(pl.multiple_of(row_dev(dy, dx)[0] * 32, 32), 32)

    my_share = pl.ds(pl.multiple_of(row * 32, 32), 32)

    def scatter_copy(w, n, i):
        buf, got = ((h_send, h_recv), (ga_send, ga_recv))[w]
        dy, dx = ROW_ORDER[i]
        return send(
            buf.at[n, share(dy, dx)], got.at[i, n],
            rs_s.at[w, n, i], rs_r.at[w, n, i], row_dev(dy, dx),
        )

    def gather_copy(w, n, i):
        full = (a_all, g_all)[w]
        dy, dx = ROW_ORDER[i]
        ref = full.at[n, my_share]
        return send(ref, ref, ag_s.at[w, n, i], ag_r.at[w, n, i], row_dev(dy, dx))

    def loop(body):
        lax.fori_loop(0, NCH, lambda n, c: (body(n), c)[1], 0)

    def hidden_part(n):
        h_send[n] = dot_nn(t_all[...].reshape(256, width), w1d[:, cols(n)]).astype(BF16)
        for i in range(7):
            scatter_copy(0, n, i).start()

    def grad_part(n):
        ga_send[n] = dot_nt(c_all[...].reshape(256, width), w2d[cols(n), :]).astype(BF16)
        for i in range(7):
            scatter_copy(1, n, i).start()

    def summed(w, n):
        buf, got = ((h_send, h_recv), (ga_send, ga_recv))[w]
        total = buf[n, my_share, :].astype(F32)
        for i in range(7):
            scatter_copy(w, n, i).wait_recv()
        for i in range(7):
            total = total + got[i, n].astype(F32)
        return total

    def act_part(n):
        v = summed(0, n) + bias[:, cols(n)]
        t = jnp.tanh(SLOPE * (v + 0.044715 * v * v * v))
        a_all[n, my_share, :] = (0.5 * v * (1.0 + t)).astype(BF16)
        slope_s[n] = 0.5 * (1.0 + t) + 0.5 * v * (1.0 - t * t) * SLOPE * (
            1.0 + 3.0 * 0.044715 * v * v
        )
        for i in range(7):
            gather_copy(0, n, i).start()

    def gh_part(n):
        g_all[n, my_share, :] = (summed(1, n) * slope_s[n]).astype(BF16)
        for i in range(7):
            gather_copy(1, n, i).start()

    def gathered(w):
        def body(n):
            for i in range(7):
                gather_copy(w, n, i).wait_recv()

        loop(body)

    forward_z(0)
    forward_x(0)
    finish(0)
    loop(hidden_part)
    forward_z(1)
    forward_x(1)
    finish(1)
    loop(grad_part)
    loop(act_part)
    loop(gh_part)

    def quarter(kk, xx):
        return pl.ds(pl.multiple_of(kk * 128 + xx * 64, 64), 64)

    def eighth(zz):
        return pl.ds(pl.multiple_of(zz * 8, 8), 8)

    def copy_a(w, n):
        return send(s_send.at[w, n], s_recv.at[w, n], la_s.at[w, n], la_r.at[w, n], sib)

    def copy_b(w, n):
        return send(b_send.at[w, n], b_recv.at[w, n], lb_s.at[w, n], lb_r.at[w, n], xnb)

    def copy_c(w, n, d):
        zz = (z + d) % 8
        return send(
            z_send.at[w, n, zz], z_recv.at[w, n, d], lc_s.at[w, n, d], lc_r.at[w, n, d], col_dev(zz, xl, k)
        )

    def level_a(w):
        full = (a_all, g_all)[w]

        def body(n):
            part = None
            for c in range(NCH):
                left = jnp.concatenate(
                    [full[c, quarter(kk, xx), :] for kk in (1 - k, k) for xx in (1 - xl, xl)], axis=0
                )
                deep = slice(c * cw, (c + 1) * cw)
                term = dot_nn(left, w2d[deep, cols(n)]) if w == 0 else dot_nt(left, w1d[cols(n), deep])
                part = term if part is None else part + term
            s_send[w, n] = part[:128].reshape(2, 64, cw).astype(BF16)
            own_a[w, n] = part[128:].reshape(2, 64, cw)
            copy_a(w, n).start()

        loop(body)

    def level_b(w):
        def body(n):
            copy_a(w, n).wait_recv()
            b_send[w, n] = (own_a[w, n, 0] + s_recv[w, n, 0].astype(F32)).astype(BF16)
            copy_b(w, n).start()
            own_b[w, n] = own_a[w, n, 1] + s_recv[w, n, 1].astype(F32)

        loop(body)

    def level_c(w):
        def body(n):
            copy_b(w, n).wait_recv()
            total = own_b[w, n] + b_recv[w, n].astype(F32)
            own_b[w, n] = total
            z_send[w, n] = total.reshape(8, rows, cw).astype(BF16)
            for d in Z_ORDER:
                copy_c(w, n, d).start()

        loop(body)

    def last(w):
        for n in range(NCH):
            total = own_b[w, n, eighth(z), :]
            for d in Z_WAIT:
                copy_c(w, n, d).wait_recv()
            for d in range(1, 8):
                total = total + z_recv[w, n, d].astype(F32)
            (out_o, tg_o)[w][:, n * cw:(n + 1) * cw] = total.astype(BF16)

    stores = [pltpu.make_async_copy(t_all, t_o, loc.at[4]), pltpu.make_async_copy(c_all, c_o, loc.at[5])]
    for s in stores:
        s.start()
    gathered(0)
    stores.append(pltpu.make_async_copy(a_all, a_o, loc.at[6]))
    stores[-1].start()
    level_a(0)
    level_b(0)
    gathered(1)
    stores.append(pltpu.make_async_copy(g_all, g_o, loc.at[7]))
    stores[-1].start()
    level_a(1)
    level_c(0)
    level_b(1)
    last(0)
    level_c(1)
    last(1)

    for table in (zc, xc, bc):
        for copy in table.values():
            copy.wait_send()
    for w in range(2):
        def drain(n):
            for i in range(7):
                scatter_copy(w, n, i).wait_send()
                gather_copy(w, n, i).wait_send()
            copy_a(w, n).wait_send()
            copy_b(w, n).wait_send()
            for d in range(1, 8):
                copy_c(w, n, d).wait_send()

        loop(drain)
    for s in stores:
        s.wait()


def block_grads(
    m1, m2, t, c, a, g, out_i, tg_i, g1_o, g2_o, out_o, tg_o, bg_o, i1, i2, count
):
    step = pl.program_id(0)
    per = g1_o.shape[0]

    @pl.when(step == 0)
    def _():
        out_o[...] = out_i[...]
        tg_o[...] = tg_i[...]
        bg_o[...] = jnp.concatenate(
            [jnp.sum(g[n].astype(F32), axis=0, keepdims=True) for n in range(NCH)], axis=1
        )
        for which, (mask, table) in enumerate(((m1, i1), (m2, i2))):
            tr, tc = mask.shape

            def one_row(i, slot):
                for j in range(tc):
                    table[slot] = i * tc + j
                    slot = slot + mask[i, j]
                return slot

            count[which] = lax.fori_loop(0, tr, one_row, jnp.int32(0))

    def flat(ref, i):
        return ref[:, pl.ds(pl.multiple_of(i * BLK, BLK), BLK)]

    def chunked(ref, i):
        each = ref.shape[2] // BLK
        return ref[i // each, :, pl.ds(pl.multiple_of(i % each * BLK, BLK), BLK)]

    def one_slot(s, carry):
        slot = step * per + s
        for which, (mask, table, dest) in enumerate(((m1, i1, g1_o), (m2, i2, g2_o))):
            tc = mask.shape[1]
            live = slot < count[which]
            place = jnp.where(live, table[slot], 0)
            r, q = place // tc, place % tc
            lb, rb = (flat(t, r), chunked(g, q)) if which == 0 else (chunked(a, r), flat(c, q))
            grad = lax.dot_general(lb, rb, (((0,), (0,)), ((), ())), preferred_element_type=F32)
            dest[s] = jnp.where(live, grad, 0.0)
        return carry

    lax.fori_loop(0, per, one_slot, 0, unroll=True)


def local(tokens, cotangent, w1_mask, w1_blocks, bias, w2_mask, w2_blocks):
    rows, width = tokens.shape
    total = 256
    cap = w1_blocks.shape[2]
    w1b = w1_blocks.reshape(w1_blocks.shape[2:])
    w2b = w2_blocks.reshape(w2_blocks.shape[2:])
    wide = bias.astype(F32).reshape(1, -1)
    vmem = pl.BlockSpec(memory_space=pltpu.VMEM)
    smem = pl.BlockSpec(memory_space=pltpu.SMEM)
    anyw = pl.BlockSpec(memory_space=pl.ANY)
    full = jax.ShapeDtypeStruct((NCH, total, width // NCH), BF16)
    small = jax.ShapeDtypeStruct((rows, width), BF16)
    dma = pltpu.SemaphoreType.DMA
    V = pltpu.VMEM
    cw = width // NCH
    tall = jax.ShapeDtypeStruct((total // rows, rows, width), BF16)
    out, tg, t, c, a, g = pl.pallas_call(
        mega,
        name="mega",
        out_shape=(small, small, tall, tall, full, full),
        in_specs=[vmem, vmem, smem, smem, vmem, anyw, anyw],
        out_specs=(vmem, vmem, anyw, anyw, anyw, anyw),
        scratch_shapes=[
            V((total // rows, rows, width), BF16), V((total // rows, rows, width), BF16),
            V((NCH, total, cw), BF16), V((NCH, total, cw), BF16),
            V((width, width), BF16), V((width, width), BF16),
            V((cap, BLK, BLK), BF16), V((cap, BLK, BLK), BF16),
            V((NCH, total, cw), BF16), V((NCH, total, cw), BF16),
            V((7, NCH, 32, cw), BF16), V((7, NCH, 32, cw), BF16), V((NCH, 32, cw), F32),
            V((2, NCH, 2, 64, cw), BF16), V((2, NCH, 2, 64, cw), BF16), V((2, NCH, 2, 64, cw), F32),
            V((2, NCH, 64, cw), BF16), V((2, NCH, 64, cw), BF16), V((2, NCH, 64, cw), F32),
            V((2, NCH, 8, rows, cw), BF16), V((2, NCH, 8, rows, cw), BF16),
            dma((8,)), dma((2, 8)), dma((2, 8)), dma((2, 8)), dma((2, 8)), dma((2, 16)), dma((2, 16)),
            dma((2, NCH, 7)), dma((2, NCH, 7)), dma((2, NCH, 7)), dma((2, NCH, 7)),
            dma((2, NCH)), dma((2, NCH)), dma((2, NCH)), dma((2, NCH)), dma((2, NCH, 8)), dma((2, NCH, 8)),
        ],
        compiler_params=pltpu.CompilerParams(
            collective_id=0, has_side_effects=True, vmem_limit_bytes=48 * 1024 * 1024
        ),
    )(tokens, cotangent, w1_mask, w2_mask, wide, w1b, w2b)

    per = 8
    whole = lambda shape: pl.BlockSpec(shape, lambda i: tuple(0 for _ in shape))
    mask_spec = smem
    slot_spec = pl.BlockSpec((per, BLK, BLK), lambda i: (i, 0, 0))
    grads = jax.ShapeDtypeStruct((cap, BLK, BLK), F32)
    g1, g2, out, tg, bg = pl.pallas_call(
        block_grads,
        name="block_grads",
        grid=(cap // per,),
        out_shape=(grads, grads, small, small, jax.ShapeDtypeStruct((1, width), F32)),
        in_specs=[mask_spec, mask_spec] + [whole((total, width))] * 2 + [whole((NCH, total, cw))] * 2 + [whole((rows, width))] * 2,
        out_specs=(slot_spec, slot_spec, whole((rows, width)), whole((rows, width)), whole((1, width))),
        scratch_shapes=[
            pltpu.SMEM((cap + 8,), jnp.int32), pltpu.SMEM((cap + 8,), jnp.int32), pltpu.SMEM((2,), jnp.int32)
        ],
    )(w1_mask, w2_mask, t.reshape(total, width), c.reshape(total, width), a, g, out, tg)
    return out, tg, g1[None, None], g2[None, None], bg.reshape(-1)


def solution(mesh):
    weights = P("row", "col", None, None, None)
    return jax.shard_map(
        local,
        mesh=mesh,
        in_specs=(P("col", "row"), P("col", "row"), P("row", "col"), weights, P("col"), P("col", "row"), weights),
        out_specs=(P("col", "row"), P("col", "row"), weights, weights, P("col")),
        check_vma=False,
    )
```

```python
import functools
import math

import jax
import jax.numpy as jnp
from jax import lax
from jax.experimental import pallas as pl
from jax.experimental.pallas import tpu as pltpu
from jax.sharding import PartitionSpec as P

MESH = pl.DeviceIdType.MESH
BLK = 128
NCH = 3
F32 = jnp.float32
BF16 = jnp.bfloat16
SLOPE = math.sqrt(2.0 / math.pi)
Z_ORDER = (4, 3, 5, 2, 6, 1, 7)
Z_WAIT = (1, 7, 2, 6, 3, 5, 4)
ROW_ORDER = ((2, 1), (1, 1), (3, 1), (0, 1), (2, 0), (1, 0), (3, 0))


def dot_nn(a, b):
    return jnp.dot(a, b, preferred_element_type=F32)


def dot_nt(a, b):
    return lax.dot_general(a, b, (((1,), (1,)), ((), ())), preferred_element_type=F32)


def mega(
    tok, cot, m1, m2, bias, w1, w2,
    out_o, tg_o, t_o, c_o, a_o, g_o,
    t_all, c_all, a_all, g_all, w1d, w2d, wb1, wb2,
    h_send, ga_send, h_recv, ga_recv, slope_s,
    bias_s, s_send, s_recv, own_a, b_send, b_recv, own_b, z_send, z_recv, t_turn, a_turn,
    loc, zs, zr, xs, xr, bs, br, rs_s, rs_r, ag_s, ag_r, la_s, la_r, lb_s, lb_r, lc_s, lc_r,
):
    rows = tok.shape[0]
    width = tok.shape[1]
    cw = width // NCH
    row, col = lax.axis_index("row"), lax.axis_index("col")
    y, xh = row // 2, row % 2
    z, xl, k = col // 4, (col // 2) % 2, col % 2

    def col_dev(zz, xx, kk):
        return (row, zz * 4 + xx * 2 + kk)

    def row_dev(dy, dx):
        return (((y + dy) % 4) * 2 + (xh + dx) % 2, col)

    def at_pos(zz, xx, kk):
        return kk * 16 + xx * 8 + zz

    def send(src, dst, ssem, rsem, dev):
        return pltpu.make_async_remote_copy(
            src_ref=src, dst_ref=dst, send_sem=ssem, recv_sem=rsem, device_id=dev, device_id_type=MESH
        )

    sib = col_dev(z, xl, 1 - k)
    xnb = col_dev(z, 1 - xl, k)
    peers = [row_dev(dy, dx) for dy, dx in ROW_ORDER]
    peers += [col_dev((z + d) % 8, xl, k) for d in range(1, 8)] + [sib, xnb]

    load1 = pltpu.make_async_copy(w1, wb1, loc.at[0])
    load2 = pltpu.make_async_copy(w2, wb2, loc.at[1])
    load1.start()
    load2.start()
    bar = pltpu.get_barrier_semaphore()
    for dev in peers:
        pl.semaphore_signal(bar, inc=1, device_id=dev, device_id_type=MESH)

    def densify(mask, blocks, dense):
        cap = blocks.shape[0]
        tr, tc = mask.shape

        def one_row(i, slot):
            for j in range(tc):
                live = mask[i, j]
                block = blocks[jnp.minimum(slot, cap - 1)]
                dense[pl.ds(pl.multiple_of(i * BLK, BLK), BLK), j * BLK:(j + 1) * BLK] = jnp.where(
                    live > 0, block, jnp.zeros_like(block)
                )
                slot = slot + live
            return slot

        lax.fori_loop(0, tr, one_row, jnp.int32(0))

    load1.wait()
    densify(m1, wb1, w1d)
    pl.semaphore_wait(bar, len(peers))

    pend = []

    ins, fulls = (tok, cot), (t_all, c_all)
    mine = at_pos(z, xl, k)
    zc, xc, bc, own = {}, {}, {}, {}
    for a in range(2):
        src, full = ins[a], fulls[a]
        for d in Z_ORDER:
            zc[a, d] = send(src, full.at[mine], zs.at[a, d], zr.at[a, d], col_dev((z + d) % 8, xl, k))
            zc[a, d].start()
        xc[a, 0] = send(src, full.at[mine], xs.at[a, 0], xr.at[a, 0], xnb)
        xc[a, 0].start()
        bc[a, 0] = send(src, full.at[mine], bs.at[a, 0], br.at[a, 0], sib)
        bc[a, 0].start()
        own[a] = pltpu.make_async_copy(src, full.at[mine], loc.at[2 + a])
        own[a].start()
    bias_s[...] = bias[...].astype(F32).reshape(1, width)
    load2.wait()
    densify(m2, wb2, w2d)

    def forward_z(a):
        full = fulls[a]
        for d in Z_WAIT:
            zc[a, d].wait_recv()
            got = full.at[at_pos((z - d + 8) % 8, xl, k)]
            xc[a, d] = send(got, got, xs.at[a, d], xr.at[a, d], xnb)
            xc[a, d].start()
            bc[a, d] = send(got, got, bs.at[a, d], br.at[a, d], sib)
            bc[a, d].start()

    def forward_x(a):
        full = fulls[a]
        for d in (0,) + Z_WAIT:
            xc[a, d].wait_recv()
            got = full.at[at_pos((z - d + 8) % 8, 1 - xl, k)]
            bc[a, 8 + d] = send(got, got, bs.at[a, 8 + d], br.at[a, 8 + d], sib)
            bc[a, 8 + d].start()

    def finish(a):
        own[a].wait()
        for d in range(16):
            bc[a, d].wait_recv()

    def cols(n):
        return pl.ds(pl.multiple_of(n * cw, cw), cw)

    def share(dy, dx):
        return pl.ds(pl.multiple_of(row_dev(dy, dx)[0] * 32, 32), 32)

    my_share = pl.ds(pl.multiple_of(row * 32, 32), 32)

    def scatter_copy(w, n, i):
        buf, got = ((h_send, h_recv), (ga_send, ga_recv))[w]
        dy, dx = ROW_ORDER[i]
        return send(
            buf.at[n, share(dy, dx)], got.at[i, n],
            rs_s.at[w, n, i], rs_r.at[w, n, i], row_dev(dy, dx),
        )

    def gather_copy(w, n, i):
        full = (a_all, g_all)[w]
        dy, dx = ROW_ORDER[i]
        ref = full.at[n, my_share]
        return send(ref, ref, ag_s.at[w, n, i], ag_r.at[w, n, i], row_dev(dy, dx))

    def loop(body):
        lax.fori_loop(0, NCH, lambda n, c: (body(n), c)[1], 0)

    def hidden_part(n):
        h_send[n] = dot_nn(t_all[...].reshape(256, width), w1d[:, cols(n)]).astype(BF16)
        for i in range(7):
            scatter_copy(0, n, i).start()

    def grad_part(n):
        ga_send[n] = dot_nt(c_all[...].reshape(256, width), w2d[cols(n), :]).astype(BF16)
        for i in range(7):
            scatter_copy(1, n, i).start()

    def summed(w, n):
        buf, got = ((h_send, h_recv), (ga_send, ga_recv))[w]
        total = buf[n, my_share, :].astype(F32)
        for i in range(7):
            scatter_copy(w, n, i).wait_recv()
        for i in range(7):
            total = total + got[i, n].astype(F32)
        return total

    def act_part(n):
        v = summed(0, n) + bias_s[:, cols(n)]
        t = jnp.tanh(SLOPE * (v + 0.044715 * v * v * v))
        a_all[n, my_share, :] = (0.5 * v * (1.0 + t)).astype(BF16)
        slope_s[n] = 0.5 * (1.0 + t) + 0.5 * v * (1.0 - t * t) * SLOPE * (
            1.0 + 3.0 * 0.044715 * v * v
        )
        for i in range(7):
            gather_copy(0, n, i).start()

    def gh_part(n):
        g_all[n, my_share, :] = (summed(1, n) * slope_s[n]).astype(BF16)
        for i in range(7):
            gather_copy(1, n, i).start()

    def gathered(w):
        def body(n):
            for i in range(7):
                gather_copy(w, n, i).wait_recv()

        loop(body)

    stores = []

    def store(src, dst):
        stores.append(pltpu.make_async_copy(src, dst, loc.at[4 + len(stores)]))
        stores[-1].start()

    def turn(n):
        t_turn[pl.ds(pl.multiple_of(n * cw, cw), cw), :] = (
            t_all[:, :, cols(n)].reshape(256, cw).astype(F32).T.astype(BF16)
        )

    def turn_act(n):
        a_turn[pl.ds(pl.multiple_of(n * cw, cw), cw), :] = a_all[n].astype(F32).T.astype(BF16)

    forward_z(0)
    forward_x(0)
    forward_z(1)
    finish(0)
    loop(hidden_part)
    forward_x(1)
    finish(1)
    loop(grad_part)
    loop(turn)
    store(t_turn, t_o)
    store(c_all, c_o)
    loop(act_part)
    loop(gh_part)

    def quarter(kk, xx):
        return pl.ds(pl.multiple_of(kk * 128 + xx * 64, 64), 64)

    def eighth(zz):
        return pl.ds(pl.multiple_of(zz * 8, 8), 8)

    def copy_a(w, n):
        return send(s_send.at[w, n], s_recv.at[w, n], la_s.at[w, n], la_r.at[w, n], sib)

    def copy_b(w, n):
        return send(b_send.at[w, n], b_recv.at[w, n], lb_s.at[w, n], lb_r.at[w, n], xnb)

    def copy_c(w, n, d):
        zz = (z + d) % 8
        return send(
            z_send.at[w, n, zz], z_recv.at[w, n, d], lc_s.at[w, n, d], lc_r.at[w, n, d], col_dev(zz, xl, k)
        )

    def level_a(w):
        full = (a_all, g_all)[w]

        def body(n):
            part = None
            for c in range(NCH):
                left = jnp.concatenate(
                    [full[c, quarter(kk, xx), :] for kk in (1 - k, k) for xx in (1 - xl, xl)], axis=0
                )
                deep = slice(c * cw, (c + 1) * cw)
                term = dot_nn(left, w2d[deep, cols(n)]) if w == 0 else dot_nt(left, w1d[cols(n), deep])
                part = term if part is None else part + term
            s_send[w, n] = part[:128].reshape(2, 64, cw).astype(BF16)
            own_a[w, n] = part[128:].reshape(2, 64, cw)
            copy_a(w, n).start()

        loop(body)

    def level_b(w):
        def body(n):
            copy_a(w, n).wait_recv()
            b_send[w, n] = (own_a[w, n, 0] + s_recv[w, n, 0].astype(F32)).astype(BF16)
            copy_b(w, n).start()
            own_b[w, n] = own_a[w, n, 1] + s_recv[w, n, 1].astype(F32)

        loop(body)

    def level_c(w):
        def body(n):
            copy_b(w, n).wait_recv()
            total = own_b[w, n] + b_recv[w, n].astype(F32)
            own_b[w, n] = total
            z_send[w, n] = total.reshape(8, rows, cw).astype(BF16)
            for d in Z_ORDER:
                copy_c(w, n, d).start()

        loop(body)

    def last(w):
        for n in range(NCH):
            total = own_b[w, n, eighth(z), :]
            for d in Z_WAIT:
                copy_c(w, n, d).wait_recv()
            for d in range(1, 8):
                total = total + z_recv[w, n, d].astype(F32)
            (out_o, tg_o)[w][:, n * cw:(n + 1) * cw] = total.astype(BF16)

    gathered(0)
    level_a(0)
    level_b(0)
    loop(turn_act)
    store(a_turn, a_o)
    gathered(1)
    level_a(1)
    store(g_all, g_o)
    level_c(0)
    level_b(1)
    level_c(1)
    last(0)
    last(1)

    for table in (zc, xc, bc):
        for copy in table.values():
            copy.wait_send()
    for w in range(2):
        def drain(n):
            for i in range(7):
                scatter_copy(w, n, i).wait_send()
                gather_copy(w, n, i).wait_send()
            copy_a(w, n).wait_send()
            copy_b(w, n).wait_send()
            for d in range(1, 8):
                copy_c(w, n, d).wait_send()

        loop(drain)
    for s in stores:
        s.wait()


def block_grads(
    m1, m2, t_h, c_h, a_h, g_h, out_i, tg_i, g1_o, g2_o, out_o, tg_o, bg_o, t, c, a, g, i1, i2, count, sems
):
    step = pl.program_id(0)
    per = g1_o.shape[0]

    @pl.when(step == 0)
    def _():
        loads = [
            pltpu.make_async_copy(src, dst, sems.at[i])
            for i, (src, dst) in enumerate(((g_h, g), (t_h, t), (a_h, a), (c_h, c)))
        ]
        for load in loads:
            load.start()
        out_o[...] = out_i[...]
        tg_o[...] = tg_i[...]
        for which, (mask, table) in enumerate(((m1, i1), (m2, i2))):
            tr, tc = mask.shape

            def one_row(i, slot):
                for j in range(tc):
                    table[slot] = i * tc + j
                    slot = slot + mask[i, j]
                return slot

            count[which] = lax.fori_loop(0, tr, one_row, jnp.int32(0))
        for load in loads:
            load.wait()
        cw = g.shape[2]
        for n in range(NCH):
            bg_o[n * cw:(n + 1) * cw] = jnp.sum(g[n].astype(F32), axis=0)

    def tall(ref, i):
        return ref[pl.ds(pl.multiple_of(i * BLK, BLK), BLK), :]

    def cot(i):
        return c[:, :, pl.ds(pl.multiple_of(i * BLK, BLK), BLK)].reshape(256, BLK)

    def hid(i):
        each = g.shape[2] // BLK
        return g[i // each, :, pl.ds(pl.multiple_of(i % each * BLK, BLK), BLK)]

    for s in range(per):
        slot = step * per + s
        for which, (mask, table, dest) in enumerate(((m1, i1, g1_o), (m2, i2, g2_o))):
            tc = mask.shape[1]
            live = slot < count[which]
            place = jnp.where(live, table[slot], 0)
            r, q = place // tc, place % tc
            grad = dot_nn(tall(t, r), hid(q)) if which == 0 else dot_nn(tall(a, r), cot(q))
            dest[s] = jnp.where(live, grad, 0.0)


def local(tokens, cotangent, w1_mask, w1_blocks, bias, w2_mask, w2_blocks):
    rows, width = tokens.shape
    total = 256
    cap = w1_blocks.shape[2]
    w1b = w1_blocks.reshape(w1_blocks.shape[2:])
    w2b = w2_blocks.reshape(w2_blocks.shape[2:])
    vmem = pl.BlockSpec(memory_space=pltpu.VMEM)
    smem = pl.BlockSpec(memory_space=pltpu.SMEM)
    anyw = pl.BlockSpec(memory_space=pl.ANY)
    full = jax.ShapeDtypeStruct((NCH, total, width // NCH), BF16)
    small = jax.ShapeDtypeStruct((rows, width), BF16)
    dma = pltpu.SemaphoreType.DMA
    V = pltpu.VMEM
    cw = width // NCH
    turned = jax.ShapeDtypeStruct((width, total), BF16)
    tall = jax.ShapeDtypeStruct((total // rows, rows, width), BF16)
    out, tg, t, c, a, g = pl.pallas_call(
        mega,
        name="mega",
        out_shape=(small, small, turned, tall, turned, full),
        in_specs=[vmem, vmem, smem, smem, vmem, anyw, anyw],
        out_specs=(vmem, vmem, anyw, anyw, anyw, anyw),
        scratch_shapes=[
            V((total // rows, rows, width), BF16), V((total // rows, rows, width), BF16),
            V((NCH, total, cw), BF16), V((NCH, total, cw), BF16),
            V((width, width), BF16), V((width, width), BF16),
            V((cap, BLK, BLK), BF16), V((cap, BLK, BLK), BF16),
            V((NCH, total, cw), BF16), V((NCH, total, cw), BF16),
            V((7, NCH, 32, cw), BF16), V((7, NCH, 32, cw), BF16), V((NCH, 32, cw), F32), V((1, width), F32),
            V((2, NCH, 2, 64, cw), BF16), V((2, NCH, 2, 64, cw), BF16), V((2, NCH, 2, 64, cw), F32),
            V((2, NCH, 64, cw), BF16), V((2, NCH, 64, cw), BF16), V((2, NCH, 64, cw), F32),
            V((2, NCH, 8, rows, cw), BF16), V((2, NCH, 8, rows, cw), BF16), V((width, total), BF16), V((width, total), BF16),
            dma((8,)), dma((2, 8)), dma((2, 8)), dma((2, 8)), dma((2, 8)), dma((2, 16)), dma((2, 16)),
            dma((2, NCH, 7)), dma((2, NCH, 7)), dma((2, NCH, 7)), dma((2, NCH, 7)),
            dma((2, NCH)), dma((2, NCH)), dma((2, NCH)), dma((2, NCH)), dma((2, NCH, 8)), dma((2, NCH, 8)),
        ],
        compiler_params=pltpu.CompilerParams(
            collective_id=0, has_side_effects=True, vmem_limit_bytes=67043328
        ),
    )(tokens, cotangent, w1_mask, w2_mask, bias, w1b, w2b)

    per = 8
    whole = lambda shape: pl.BlockSpec(shape, lambda i: tuple(0 for _ in shape))
    mask_spec = smem
    slot_spec = pl.BlockSpec((per, BLK, BLK), lambda i: (i, 0, 0))
    grads = jax.ShapeDtypeStruct((cap, BLK, BLK), F32)
    g1, g2, out, tg, bg = pl.pallas_call(
        block_grads,
        name="block_grads",
        grid=(cap // per,),
        out_shape=(grads, grads, small, small, jax.ShapeDtypeStruct((width,), F32)),
        in_specs=[mask_spec, mask_spec] + [anyw] * 4 + [whole((rows, width))] * 2,
        out_specs=(slot_spec, slot_spec, whole((rows, width)), whole((rows, width)), whole((width,))),
        scratch_shapes=[
            V((width, total), BF16), V((total // rows, rows, width), BF16),
            V((width, total), BF16), V((NCH, total, cw), BF16),
            pltpu.SMEM((cap + 8,), jnp.int32), pltpu.SMEM((cap + 8,), jnp.int32), pltpu.SMEM((2,), jnp.int32),
            dma((4,)),
        ],
        compiler_params=pltpu.CompilerParams(vmem_limit_bytes=67043328),
    )(w1_mask, w2_mask, t, c, a, g, out, tg)
    return out, tg, g1[None, None], g2[None, None], bg


def solution(mesh):
    weights = P("row", "col", None, None, None)
    return jax.shard_map(
        local,
        mesh=mesh,
        in_specs=(P("col", "row"), P("col", "row"), P("row", "col"), weights, P("col"), P("col", "row"), weights),
        out_specs=(P("col", "row"), P("col", "row"), weights, weights, P("col")),
        check_vma=False,
    )
```

```python
import functools
import math

import jax
import jax.numpy as jnp
from jax import lax
from jax.experimental import pallas as pl
from jax.experimental.pallas import tpu as pltpu
from jax.sharding import PartitionSpec as P

MESH = pl.DeviceIdType.MESH
BLK = 128
GROUP = 4
NCH = 3
F32 = jnp.float32
BF16 = jnp.bfloat16
SLOPE = math.sqrt(2.0 / math.pi)
Z_ORDER = (4, 3, 5, 2, 6, 1, 7)
Z_WAIT = (1, 7, 2, 6, 3, 5, 4)
ROW_ORDER = ((2, 1), (1, 1), (3, 1), (0, 1), (2, 0), (1, 0), (3, 0))


def dot_nn(a, b):
    return jnp.dot(a, b, preferred_element_type=F32)


def dot_nt(a, b):
    return lax.dot_general(a, b, (((1,), (1,)), ((), ())), preferred_element_type=F32)


def mega(
    tok, cot, m1, m2, bias, w1, w2,
    out_o, tg_o, t_o, c_o, a_o, g_o,
    t_all, c_all, a_all, g_all, w1d, w2d, wb1, wb2,
    h_send, ga_send, h_recv, ga_recv, slope_s, bias_s,
    a_send, a_recv, own_there, own_here, b_send, b_recv, z_send, z_recv, t_turn, a_turn,
    loc, zs, zr, xs, xr, bs, br, rs_s, rs_r, ag_s, ag_r, la_s, la_r, lb_s, lb_r, lc_s, lc_r,
):
    width = tok.shape[1]
    cw = width // NCH
    row, col = lax.axis_index("row"), lax.axis_index("col")
    y, xh = row // 2, row % 2
    z, xl, k = col // 4, (col // 2) % 2, col % 2

    def col_dev(zz, xx, kk):
        return (row, zz * 4 + xx * 2 + kk)

    def row_dev(dy, dx):
        return (((y + dy) % 4) * 2 + (xh + dx) % 2, col)

    def back(d):
        return (z - d + 8) % 8

    def send(src, dst, ssem, rsem, dev):
        return pltpu.make_async_remote_copy(
            src_ref=src, dst_ref=dst, send_sem=ssem, recv_sem=rsem, device_id=dev, device_id_type=MESH
        )

    sib = col_dev(z, xl, 1 - k)
    xnb = col_dev(z, 1 - xl, k)
    peers = [row_dev(dy, dx) for dy, dx in ROW_ORDER]
    peers += [col_dev((z + d) % 8, xl, k) for d in range(1, 8)] + [sib, xnb]

    load1 = pltpu.make_async_copy(w1, wb1, loc.at[0])
    load2 = pltpu.make_async_copy(w2, wb2, loc.at[1])
    load1.start()
    load2.start()
    bar = pltpu.get_barrier_semaphore()
    for dev in peers:
        pl.semaphore_signal(bar, inc=1, device_id=dev, device_id_type=MESH)

    def densify(mask, blocks, dense):
        cap = blocks.shape[0]
        tr, tc = mask.shape

        def one_row(i, slot):
            for j in range(tc):
                live = mask[i, j]
                block = blocks[jnp.minimum(slot, cap - 1)]
                dense[pl.ds(pl.multiple_of(i * BLK, BLK), BLK), j * BLK:(j + 1) * BLK] = jnp.where(
                    live > 0, block, jnp.zeros_like(block)
                )
                slot = slot + live
            return slot

        lax.fori_loop(0, tr, one_row, jnp.int32(0))

    load1.wait()
    densify(m1, wb1, w1d)
    pl.semaphore_wait(bar, len(peers))

    ins, fulls = (tok, cot), (t_all, c_all)
    zc, xc, bc, own = {}, {}, {}, {}
    for a in range(2):
        src, full = ins[a], fulls[a]
        for d in Z_ORDER:
            zc[a, d] = send(src, full.at[0, z], zs.at[a, d], zr.at[a, d], col_dev((z + d) % 8, xl, k))
            zc[a, d].start()
        xc[a, 0] = send(src, full.at[2, z], xs.at[a, 0], xr.at[a, 0], xnb)
        xc[a, 0].start()
        bc[a, 0] = send(src, full.at[1, z], bs.at[a, 0], br.at[a, 0], sib)
        bc[a, 0].start()
        own[a] = pltpu.make_async_copy(src, full.at[0, z], loc.at[2 + a])
        own[a].start()
    bias_s[...] = bias[...].astype(F32).reshape(1, width)
    load2.wait()
    densify(m2, wb2, w2d)

    def forward_z(a):
        full = fulls[a]
        for d in Z_WAIT:
            zc[a, d].wait_recv()
            got = full.at[0, back(d)]
            xc[a, d] = send(got, full.at[2, back(d)], xs.at[a, d], xr.at[a, d], xnb)
            xc[a, d].start()
            bc[a, d] = send(got, full.at[1, back(d)], bs.at[a, d], br.at[a, d], sib)
            bc[a, d].start()
        own[a].wait()

    def forward_x(a):
        full = fulls[a]
        for d in (0,) + Z_WAIT:
            xc[a, d].wait_recv()
            bc[a, 8 + d] = send(
                full.at[2, back(d)], full.at[3, back(d)], bs.at[a, 8 + d], br.at[a, 8 + d], sib
            )
            bc[a, 8 + d].start()

    def arrived(a, first):
        for d in range(first, first + 8):
            bc[a, d].wait_recv()

    def cols(n):
        return pl.ds(pl.multiple_of(n * cw, cw), cw)

    def loop(body):
        lax.fori_loop(0, NCH, lambda n, c: (body(n), c)[1], 0)

    def scatter_copy(w, q, i):
        buf, got = ((h_send, h_recv), (ga_send, ga_recv))[w]
        dev = row_dev(*ROW_ORDER[i])
        return send(buf.at[q, dev[0]], got.at[q, i], rs_s.at[w, q, i], rs_r.at[w, q, i], dev)

    def gather_copy(w, q, i):
        ref = (a_all, g_all)[w].at[q, row]
        return send(ref, ref, ag_s.at[w, q, i], ag_r.at[w, q, i], row_dev(*ROW_ORDER[i]))

    def scatter(w, quarters):
        full, buf = ((t_all, h_send), (c_all, ga_send))[w]

        def body(n):
            left = jnp.concatenate([full[q].reshape(64, width) for q in quarters], axis=0)
            part = dot_nn(left, w1d[:, cols(n)]) if w == 0 else dot_nt(left, w2d[cols(n), :])
            for at, q in enumerate(quarters):
                buf[q, :, :, cols(n)] = part[at * 64:(at + 1) * 64].reshape(8, 8, cw).astype(BF16)

        loop(body)
        for q in quarters:
            for i in range(7):
                scatter_copy(w, q, i).start()

    def summed(w, q):
        buf, got = ((h_send, h_recv), (ga_send, ga_recv))[w]
        total = buf[q, row].astype(F32)
        for i in range(7):
            scatter_copy(w, q, i).wait_recv()
        for i in range(7):
            total = total + got[q, i].astype(F32)
        return total

    def spread(w, q, value):
        (a_all, g_all)[w][q, row] = value.astype(BF16)
        for i in range(7):
            gather_copy(w, q, i).start()

    def act_part(q):
        v = summed(0, q) + bias_s[...]
        t = jnp.tanh(SLOPE * (v + 0.044715 * v * v * v))
        spread(0, q, 0.5 * v * (1.0 + t))
        slope_s[q] = 0.5 * (1.0 + t) + 0.5 * v * (1.0 - t * t) * SLOPE * (
            1.0 + 3.0 * 0.044715 * v * v
        )

    def gh_part(q):
        spread(1, q, summed(1, q) * slope_s[q])

    stores = []

    def store(src, dst):
        stores.append(pltpu.make_async_copy(src, dst, loc.at[4 + len(stores)]))
        stores[-1].start()

    def turn(src, dst):
        def body(n):
            dst[cols(n), :] = src[:, :, :, cols(n)].reshape(256, cw).astype(F32).T.astype(BF16)

        loop(body)

    def copy_a(w, part):
        return send(a_send.at[w, part], a_recv.at[w, part], la_s.at[w, part], la_r.at[w, part], sib)

    def copy_b(w):
        return send(b_send.at[w], b_recv.at[w], lb_s.at[w], lb_r.at[w], xnb)

    def copy_c(w, d):
        zz = (z + d) % 8
        return send(z_send.at[w, zz], z_recv.at[w, d], lc_s.at[w, d], lc_r.at[w, d], col_dev(zz, xl, k))

    def project(w, q, put):
        full = (a_all, g_all)[w]
        for i in range(7):
            gather_copy(w, q, i).wait_recv()

        def body(n):
            left = full[q].reshape(64, width)
            part = dot_nn(left, w2d[:, cols(n)]) if w == 0 else dot_nt(left, w1d[cols(n), :])
            put(n, part.reshape(8, 8, cw))

        loop(body)

    def to_sibling(w, part, q):
        def put(n, value):
            a_send[w, part, :, :, cols(n)] = value.astype(BF16)

        project(w, q, put)
        copy_a(w, part).start()

    def far_half(w):
        to_sibling(w, 0, 3)

        def put(n, value):
            own_there[:, :, cols(n)] = value

        project(w, 2, put)
        copy_a(w, 0).wait_recv()
        b_send[w] = (own_there[...] + a_recv[w, 0].astype(F32)).astype(BF16)
        copy_b(w).start()

    def near_half(w):
        to_sibling(w, 1, 1)

        def put(n, value):
            own_here[w, :, :, cols(n)] = value

        project(w, 0, put)

    def over_z(w):
        copy_a(w, 1).wait_recv()
        copy_b(w).wait_recv()
        total = own_here[w] + a_recv[w, 1].astype(F32) + b_recv[w].astype(F32)
        own_here[w] = total
        z_send[w] = total.astype(BF16)
        for d in Z_ORDER:
            copy_c(w, d).start()

    def last(w):
        total = own_here[w, z]
        for d in Z_WAIT:
            copy_c(w, d).wait_recv()
        for d in range(1, 8):
            total = total + z_recv[w, d].astype(F32)
        (out_o, tg_o)[w][...] = total.astype(BF16)

    forward_z(0)
    scatter(0, (0,))
    forward_x(0)
    arrived(0, 0)
    scatter(0, (1,))
    scatter(0, (2,))
    forward_z(1)
    arrived(0, 8)
    scatter(0, (3,))
    forward_x(1)
    arrived(1, 0)
    scatter(1, (0, 1))
    arrived(1, 8)
    scatter(1, (2, 3))
    turn(t_all, t_turn)
    store(t_turn, t_o)
    store(c_all, c_o)
    for q in (3, 2, 1, 0):
        act_part(q)
    for q in (3, 2, 1, 0):
        gh_part(q)
    far_half(0)
    near_half(0)
    turn(a_all, a_turn)
    store(a_turn, a_o)
    far_half(1)
    over_z(0)
    near_half(1)
    over_z(1)
    store(g_all, g_o)
    last(0)
    last(1)

    for table in (zc, xc, bc):
        for copy in table.values():
            copy.wait_send()
    for w in range(2):
        for q in range(4):
            for i in range(7):
                scatter_copy(w, q, i).wait_send()
                gather_copy(w, q, i).wait_send()
        copy_a(w, 0).wait_send()
        copy_a(w, 1).wait_send()
        copy_b(w).wait_send()
        for d in range(1, 8):
            copy_c(w, d).wait_send()
    for s in stores:
        s.wait()


def block_grads(
    m1, m2, t_h, c_h, a_h, g_h, out_i, tg_i, g1_o, g2_o, out_o, tg_o, bg_o,
    t, c, a, g, b1, b2, i1, i2, sems, puts,
):
    width = c.shape[-1]
    groups = b1.shape[0] // GROUP
    loads = [
        pltpu.make_async_copy(src, dst, sems.at[i])
        for i, (src, dst) in enumerate(((g_h, g), (t_h, t), (a_h, a), (c_h, c)))
    ]
    for load in loads:
        load.start()
    out_o[...] = out_i[...]
    tg_o[...] = tg_i[...]
    counts = []
    for mask, table in ((m1, i1), (m2, i2)):
        tr, tc = mask.shape

        def one_row(i, slot):
            for j in range(tc):
                table[slot] = i * tc + j
                slot = slot + mask[i, j]
            return slot

        counts.append(lax.fori_loop(0, tr, one_row, jnp.int32(0)))

    def tall(ref, i):
        return ref[pl.ds(pl.multiple_of(i * BLK, BLK), BLK), :]

    def wide(ref, i):
        return ref[:, :, :, pl.ds(pl.multiple_of(i * BLK, BLK), BLK)].reshape(256, BLK)

    def put(which, at):
        src, dst = ((b1, g1_o), (b2, g2_o))[which]
        part = pl.ds(at * GROUP, GROUP)
        return pltpu.make_async_copy(src.at[part], dst.at[part], puts.at[which, at])

    for which, (left, right, mask, table, dest) in enumerate(((t, g, m1, i1, b1), (a, c, m2, i2, b2))):
        tc = mask.shape[1]
        loads[2 * which].wait()
        loads[2 * which + 1].wait()

        def one_group(at, carry):
            for u in range(GROUP):
                slot = at * GROUP + u
                live = slot < counts[which]
                place = jnp.where(live, table[slot], 0)
                grad = dot_nn(tall(left, place // tc), wide(right, place % tc))
                dest[slot] = jnp.where(live, grad, 0.0)
            put(which, at).start()
            return carry

        lax.fori_loop(0, groups, one_group, 0)
    bg_o[...] = jnp.sum(g[...].reshape(256, width).astype(F32), axis=0)
    for which in range(2):
        lax.fori_loop(0, groups, lambda at, x: (put(which, at).wait(), x)[1], 0)


def local(tokens, cotangent, w1_mask, w1_blocks, bias, w2_mask, w2_blocks):
    rows, width = tokens.shape
    total = 256
    cap = w1_blocks.shape[2]
    w1b = w1_blocks.reshape(w1_blocks.shape[2:])
    w2b = w2_blocks.reshape(w2_blocks.shape[2:])
    vmem = pl.BlockSpec(memory_space=pltpu.VMEM)
    smem = pl.BlockSpec(memory_space=pltpu.SMEM)
    anyw = pl.BlockSpec(memory_space=pl.ANY)
    small = jax.ShapeDtypeStruct((rows, width), BF16)
    turned = jax.ShapeDtypeStruct((width, total), BF16)
    quarters = (4, 8, rows, width)
    full = jax.ShapeDtypeStruct(quarters, BF16)
    dma = pltpu.SemaphoreType.DMA
    V = pltpu.VMEM
    params = dict(vmem_limit_bytes=67043328)
    out, tg, t, c, a, g = pl.pallas_call(
        mega,
        name="mega",
        out_shape=(small, small, turned, full, turned, full),
        in_specs=[vmem, vmem, smem, smem, vmem, anyw, anyw],
        out_specs=(vmem, vmem, anyw, anyw, anyw, anyw),
        scratch_shapes=[
            V(quarters, BF16), V(quarters, BF16), V(quarters, BF16), V(quarters, BF16),
            V((width, width), BF16), V((width, width), BF16),
            V((cap, BLK, BLK), BF16), V((cap, BLK, BLK), BF16),
            V(quarters, BF16), V(quarters, BF16),
            V((4, 7, rows, width), BF16), V((4, 7, rows, width), BF16),
            V((4, rows, width), F32), V((1, width), F32),
            V((2, 2, 8, rows, width), BF16), V((2, 2, 8, rows, width), BF16),
            V((8, rows, width), F32), V((2, 8, rows, width), F32),
            V((2, 8, rows, width), BF16), V((2, 8, rows, width), BF16),
            V((2, 8, rows, width), BF16), V((2, 8, rows, width), BF16),
            V((width, total), BF16), V((width, total), BF16),
            dma((8,)), dma((2, 8)), dma((2, 8)), dma((2, 8)), dma((2, 8)), dma((2, 16)), dma((2, 16)),
            dma((2, 4, 7)), dma((2, 4, 7)), dma((2, 4, 7)), dma((2, 4, 7)),
            dma((2, 2)), dma((2, 2)), dma((2,)), dma((2,)), dma((2, 8)), dma((2, 8)),
        ],
        compiler_params=pltpu.CompilerParams(collective_id=0, has_side_effects=True, **params),
    )(tokens, cotangent, w1_mask, w2_mask, bias, w1b, w2b)

    grads = jax.ShapeDtypeStruct((cap, BLK, BLK), F32)
    g1, g2, out, tg, bg = pl.pallas_call(
        block_grads,
        name="block_grads",
        out_shape=(grads, grads, small, small, jax.ShapeDtypeStruct((width,), F32)),
        in_specs=[smem, smem] + [anyw] * 4 + [vmem] * 2,
        out_specs=(anyw, anyw, vmem, vmem, vmem),
        scratch_shapes=[
            V((width, total), BF16), V(quarters, BF16), V((width, total), BF16), V(quarters, BF16),
            V((cap, BLK, BLK), F32), V((cap, BLK, BLK), F32),
            pltpu.SMEM((cap + 8,), jnp.int32), pltpu.SMEM((cap + 8,), jnp.int32),
            dma((4,)), dma((2, cap // GROUP)),
        ],
        compiler_params=pltpu.CompilerParams(**params),
    )(w1_mask, w2_mask, t, c, a, g, out, tg)
    return out, tg, g1[None, None], g2[None, None], bg


def solution(mesh):
    weights = P("row", "col", None, None, None)
    return jax.shard_map(
        local,
        mesh=mesh,
        in_specs=(P("col", "row"), P("col", "row"), P("row", "col"), weights, P("col"), P("col", "row"), weights),
        out_specs=(P("col", "row"), P("col", "row"), weights, weights, P("col")),
        check_vma=False,
    )
```

```python
import functools
import math

import jax
import jax.numpy as jnp
from jax import lax
from jax.experimental import pallas as pl
from jax.experimental.pallas import tpu as pltpu
from jax.sharding import PartitionSpec as P

MESH = pl.DeviceIdType.MESH
BLK = 128
GROUP = 8
NCH = 3
F32 = jnp.float32
BF16 = jnp.bfloat16
SLOPE = math.sqrt(2.0 / math.pi)
Z_ORDER = (4, 3, 5, 2, 6, 1, 7)
Z_WAIT = (1, 7, 2, 6, 3, 5, 4)
Y_ORDER = (2, 1, 3)


def dot_nn(a, b):
    return jnp.dot(a, b, preferred_element_type=F32)


def dot_nt(a, b):
    return lax.dot_general(a, b, (((1,), (1,)), ((), ())), preferred_element_type=F32)


def mega(
    tok, cot, m1, m2, bias, w1, w2,
    out_o, tg_o, t_o, c_o, a_o, g_o,
    t_all, c_all, a_all, g_all, w1d, w2d, wb1, wb2,
    h_send, ga_send, h_recv, ga_recv, f_send, f_recv, slope_s, bias_s,
    a_send, a_recv, own_there, own_here, b_send, b_recv, z_send, z_recv, t_turn, a_turn,
    loc, zs, zr, xs, xr, bs, br, rs_s, rs_r, fo_s, fo_r, ag_s, ag_r, la_s, la_r, lb_s, lb_r, lc_s, lc_r,
):
    width = tok.shape[1]
    cw = width // NCH
    row, col = lax.axis_index("row"), lax.axis_index("col")
    y, xh = row // 2, row % 2
    z, xl, k = col // 4, (col // 2) % 2, col % 2

    def col_dev(zz, xx, kk):
        return (row, zz * 4 + xx * 2 + kk)

    def row_dev(dy, dx):
        return (((y + dy) % 4) * 2 + (xh + dx) % 2, col)

    def back(d):
        return (z - d + 8) % 8

    def send(src, dst, ssem, rsem, dev):
        return pltpu.make_async_remote_copy(
            src_ref=src, dst_ref=dst, send_sem=ssem, recv_sem=rsem, device_id=dev, device_id_type=MESH
        )

    sib = col_dev(z, xl, 1 - k)
    xnb = col_dev(z, 1 - xl, k)
    partner = row_dev(0, 1)
    other = y * 2 + 1 - xh
    peers = [row_dev(d, 0) for d in Y_ORDER] + [partner]
    peers += [col_dev((z + d) % 8, xl, k) for d in range(1, 8)] + [sib, xnb]

    load1 = pltpu.make_async_copy(w1, wb1, loc.at[0])
    load2 = pltpu.make_async_copy(w2, wb2, loc.at[1])
    load1.start()
    load2.start()
    bar = pltpu.get_barrier_semaphore()
    for dev in peers:
        pl.semaphore_signal(bar, inc=1, device_id=dev, device_id_type=MESH)

    def densify(mask, blocks, dense):
        cap = blocks.shape[0]
        tr, tc = mask.shape

        def one_row(i, slot):
            for j in range(tc):
                live = mask[i, j]
                block = blocks[jnp.minimum(slot, cap - 1)]
                dense[pl.ds(pl.multiple_of(i * BLK, BLK), BLK), j * BLK:(j + 1) * BLK] = jnp.where(
                    live > 0, block, jnp.zeros_like(block)
                )
                slot = slot + live
            return slot

        lax.fori_loop(0, tr, one_row, jnp.int32(0))

    load1.wait()
    densify(m1, wb1, w1d)
    pl.semaphore_wait(bar, len(peers))

    ins, fulls = (tok, cot), (t_all, c_all)
    zc, xc, bc, own = {}, {}, {}, {}
    for a in range(2):
        src, full = ins[a], fulls[a]
        for d in Z_ORDER:
            zc[a, d] = send(src, full.at[0, z], zs.at[a, d], zr.at[a, d], col_dev((z + d) % 8, xl, k))
            zc[a, d].start()
        xc[a, 0] = send(src, full.at[2, z], xs.at[a, 0], xr.at[a, 0], xnb)
        xc[a, 0].start()
        bc[a, 0] = send(src, full.at[1, z], bs.at[a, 0], br.at[a, 0], sib)
        bc[a, 0].start()
        own[a] = pltpu.make_async_copy(src, full.at[0, z], loc.at[2 + a])
        own[a].start()
    bias_s[...] = bias[...].astype(F32).reshape(1, width)
    load2.wait()
    densify(m2, wb2, w2d)

    def forward_z(a):
        full = fulls[a]
        for d in Z_WAIT:
            zc[a, d].wait_recv()
            got = full.at[0, back(d)]
            xc[a, d] = send(got, full.at[2, back(d)], xs.at[a, d], xr.at[a, d], xnb)
            xc[a, d].start()
            bc[a, d] = send(got, full.at[1, back(d)], bs.at[a, d], br.at[a, d], sib)
            bc[a, d].start()
        own[a].wait()

    def forward_x(a):
        full = fulls[a]
        for d in (0,) + Z_WAIT:
            xc[a, d].wait_recv()
            bc[a, 8 + d] = send(
                full.at[2, back(d)], full.at[3, back(d)], bs.at[a, 8 + d], br.at[a, 8 + d], sib
            )
            bc[a, 8 + d].start()

    def arrived(a, first):
        for d in range(first, first + 8):
            bc[a, d].wait_recv()

    def cols(n):
        return pl.ds(pl.multiple_of(n * cw, cw), cw)

    def loop(body):
        lax.fori_loop(0, NCH, lambda n, c: (body(n), c)[1], 0)

    def scatter_copy(w, q, i):
        buf, got = ((h_send, h_recv), (ga_send, ga_recv))[w]
        dev = row_dev(Y_ORDER[i % 3], 0)
        share = dev[0] if i >= 3 else dev[0] + 1 - 2 * xh
        return send(buf.at[q, share], got.at[q, i], rs_s.at[w, q, i], rs_r.at[w, q, i], dev)

    def fold_copy(w, q):
        return send(f_send.at[w, q], f_recv.at[w, q], fo_s.at[w, q], fo_r.at[w, q], partner)

    def gather_copy(w, q, i):
        ref = (a_all, g_all)[w].at[q, row if i < 4 else other]
        dev = partner if i == 3 else row_dev(Y_ORDER[i % 4], 0)
        return send(ref, ref, ag_s.at[w, q, i], ag_r.at[w, q, i], dev)

    def scatter(w, quarters):
        full, buf = ((t_all, h_send), (c_all, ga_send))[w]

        def body(n):
            left = jnp.concatenate([full[q].reshape(64, width) for q in quarters], axis=0)
            part = dot_nn(left, w1d[:, cols(n)]) if w == 0 else dot_nt(left, w2d[cols(n), :])
            for at, q in enumerate(quarters):
                buf[q, :, :, cols(n)] = part[at * 64:(at + 1) * 64].reshape(8, 8, cw).astype(BF16)

        loop(body)
        for q in quarters:
            for i in range(6):
                scatter_copy(w, q, i).start()

    def fold(w, q):
        buf, got = ((h_send, h_recv), (ga_send, ga_recv))[w]
        for i in range(3):
            scatter_copy(w, q, i).wait_recv()
        total = buf[q, other].astype(F32)
        for i in range(3):
            total = total + got[q, i].astype(F32)
        f_send[w, q] = total.astype(BF16)
        fold_copy(w, q).start()

    def summed(w, q):
        buf, got = ((h_send, h_recv), (ga_send, ga_recv))[w]
        for i in range(3, 6):
            scatter_copy(w, q, i).wait_recv()
        fold_copy(w, q).wait_recv()
        total = buf[q, row].astype(F32) + f_recv[w, q].astype(F32)
        for i in range(3, 6):
            total = total + got[q, i].astype(F32)
        return total

    def spread(w, q, value):
        (a_all, g_all)[w][q, row] = value.astype(BF16)
        for i in (3, 0, 1, 2):
            gather_copy(w, q, i).start()

    def relay(w, q):
        gather_copy(w, q, 3).wait_recv()
        for i in (4, 5, 6):
            gather_copy(w, q, i).start()

    def act_part(q):
        v = summed(0, q) + bias_s[...]
        t = jnp.tanh(SLOPE * (v + 0.044715 * v * v * v))
        spread(0, q, 0.5 * v * (1.0 + t))
        slope_s[q] = 0.5 * (1.0 + t) + 0.5 * v * (1.0 - t * t) * SLOPE * (
            1.0 + 3.0 * 0.044715 * v * v
        )

    def gh_part(q):
        spread(1, q, summed(1, q) * slope_s[q])

    stores = []

    def store(src, dst):
        stores.append(pltpu.make_async_copy(src, dst, loc.at[4 + len(stores)]))
        stores[-1].start()

    def turn(src, dst):
        def body(n):
            dst[cols(n), :] = src[:, :, :, cols(n)].reshape(256, cw).astype(F32).T.astype(BF16)

        loop(body)

    def copy_a(w, part):
        return send(a_send.at[w, part], a_recv.at[w, part], la_s.at[w, part], la_r.at[w, part], sib)

    def copy_b(w):
        return send(b_send.at[w], b_recv.at[w], lb_s.at[w], lb_r.at[w], xnb)

    def copy_c(w, d):
        zz = (z + d) % 8
        return send(z_send.at[w, zz], z_recv.at[w, d], lc_s.at[w, d], lc_r.at[w, d], col_dev(zz, xl, k))

    def project(w, q, put):
        full = (a_all, g_all)[w]
        for i in (0, 1, 2, 4, 5, 6):
            gather_copy(w, q, i).wait_recv()

        def body(n):
            left = full[q].reshape(64, width)
            part = dot_nn(left, w2d[:, cols(n)]) if w == 0 else dot_nt(left, w1d[cols(n), :])
            put(n, part.reshape(8, 8, cw))

        loop(body)

    def to_sibling(w, part, q):
        def put(n, value):
            a_send[w, part, :, :, cols(n)] = value

        project(w, q, put)
        copy_a(w, part).start()

    def far_half(w):
        to_sibling(w, 0, 3)

        def put(n, value):
            own_there[:, :, cols(n)] = value

        project(w, 2, put)
        copy_a(w, 0).wait_recv()
        b_send[w] = (own_there[...] + a_recv[w, 0]).astype(BF16)
        copy_b(w).start()

    def near_half(w):
        to_sibling(w, 1, 1)

        def put(n, value):
            own_here[w, :, :, cols(n)] = value

        project(w, 0, put)

    def over_z(w):
        copy_a(w, 1).wait_recv()
        copy_b(w).wait_recv()
        total = own_here[w] + a_recv[w, 1] + b_recv[w].astype(F32)
        own_here[w] = total
        z_send[w] = total.astype(BF16)
        for d in Z_ORDER:
            copy_c(w, d).start()

    def last(w):
        total = own_here[w, z]
        for d in Z_WAIT:
            copy_c(w, d).wait_recv()
        for d in range(1, 8):
            total = total + z_recv[w, d].astype(F32)
        (out_o, tg_o)[w][...] = total.astype(BF16)

    forward_z(0)
    scatter(0, (0,))
    forward_x(0)
    arrived(0, 0)
    scatter(0, (1,))
    scatter(0, (2,))
    forward_z(1)
    arrived(0, 8)
    scatter(0, (3,))
    forward_x(1)
    arrived(1, 0)
    scatter(1, (0, 1))
    fold(0, 0)
    fold(0, 1)
    arrived(1, 8)
    scatter(1, (2, 3))
    fold(0, 2)
    fold(0, 3)
    for q in (3, 2, 1, 0):
        act_part(q)
    for q in (3, 2, 1, 0):
        fold(1, q)
    for q in (3, 2, 1, 0):
        relay(0, q)
    for q in (3, 2, 1, 0):
        gh_part(q)
    store(c_all, c_o)
    for q in (3, 2, 1, 0):
        relay(1, q)
    turn(t_all, t_turn)
    store(t_turn, t_o)
    far_half(0)
    near_half(0)
    turn(a_all, a_turn)
    store(a_turn, a_o)
    far_half(1)
    over_z(0)
    near_half(1)
    store(g_all, g_o)
    over_z(1)
    last(0)
    last(1)

    for table in (zc, xc, bc):
        for copy in table.values():
            copy.wait_send()
    for w in range(2):
        for q in range(4):
            for i in range(6):
                scatter_copy(w, q, i).wait_send()
            fold_copy(w, q).wait_send()
            for i in range(7):
                gather_copy(w, q, i).wait_send()
        copy_a(w, 0).wait_send()
        copy_a(w, 1).wait_send()
        copy_b(w).wait_send()
        for d in range(1, 8):
            copy_c(w, d).wait_send()
    for s in stores:
        s.wait()


def block_grads(
    m1, m2, t_h, c_h, a_h, g_h, out_i, tg_i, g1_o, g2_o, out_o, tg_o, bg_o,
    t, c, a, g, b1, b2, i1, i2, sems, puts,
):
    groups = b1.shape[0] // GROUP
    loads = [
        pltpu.make_async_copy(src, dst, sems.at[i])
        for i, (src, dst) in enumerate(((g_h, g), (t_h, t), (a_h, a), (c_h, c)))
    ]
    for load in loads:
        load.start()
    out_o[...] = out_i[...]
    tg_o[...] = tg_i[...]
    counts = []
    for mask, table in ((m1, i1), (m2, i2)):
        tr, tc = mask.shape

        def one_row(i, slot):
            for j in range(tc):
                table[slot] = i * tc + j
                slot = slot + mask[i, j]
            return slot

        counts.append(lax.fori_loop(0, tr, one_row, jnp.int32(0)))

    def tall(ref, i):
        return ref[pl.ds(pl.multiple_of(i * BLK, BLK), BLK), :]

    def wide(ref, i):
        return ref[:, pl.ds(pl.multiple_of(i * BLK, BLK), BLK)]

    def put(which, at):
        src, dst = ((b1, g1_o), (b2, g2_o))[which]
        part = pl.ds(at * GROUP, GROUP)
        return pltpu.make_async_copy(src.at[part], dst.at[part], puts.at[which, at])

    for which, (left, right, mask, table, dest) in enumerate(((t, g, m1, i1, b1), (a, c, m2, i2, b2))):
        tc = mask.shape[1]
        loads[2 * which].wait()
        loads[2 * which + 1].wait()

        def one_group(at, carry):
            for u in range(GROUP):
                slot = at * GROUP + u
                live = slot < counts[which]
                place = jnp.where(live, table[slot], 0)
                grad = dot_nn(tall(left, place // tc), wide(right, place % tc))
                dest[slot] = jnp.where(live, grad, 0.0)
            put(which, at).start()
            return carry

        lax.fori_loop(0, groups, one_group, 0)
    bg_o[...] = jnp.sum(g[...].astype(F32), axis=0)
    for which in range(2):
        lax.fori_loop(0, groups, lambda at, x: (put(which, at).wait(), x)[1], 0)


def local(tokens, cotangent, w1_mask, w1_blocks, bias, w2_mask, w2_blocks):
    rows, width = tokens.shape
    total = 256
    cap = w1_blocks.shape[2]
    w1b = w1_blocks.reshape(w1_blocks.shape[2:])
    w2b = w2_blocks.reshape(w2_blocks.shape[2:])
    vmem = pl.BlockSpec(memory_space=pltpu.VMEM)
    smem = pl.BlockSpec(memory_space=pltpu.SMEM)
    anyw = pl.BlockSpec(memory_space=pl.ANY)
    small = jax.ShapeDtypeStruct((rows, width), BF16)
    turned = jax.ShapeDtypeStruct((width, total), BF16)
    quarters = (4, 8, rows, width)
    full = jax.ShapeDtypeStruct(quarters, BF16)
    dma = pltpu.SemaphoreType.DMA
    V = pltpu.VMEM
    params = dict(vmem_limit_bytes=67043328)
    out, tg, t, c, a, g = pl.pallas_call(
        mega,
        name="mega",
        out_shape=(small, small, turned, full, turned, full),
        in_specs=[vmem, vmem, smem, smem, vmem, anyw, anyw],
        out_specs=(vmem, vmem, anyw, anyw, anyw, anyw),
        scratch_shapes=[
            V(quarters, BF16), V(quarters, BF16), V(quarters, BF16), V(quarters, BF16),
            V((width, width), BF16), V((width, width), BF16),
            V((cap, BLK, BLK), BF16), V((cap, BLK, BLK), BF16),
            V(quarters, BF16), V(quarters, BF16),
            V((4, 6, rows, width), BF16), V((4, 6, rows, width), BF16),
            V((2, 4, rows, width), BF16), V((2, 4, rows, width), BF16),
            V((4, rows, width), F32), V((1, width), F32),
            V((2, 2, 8, rows, width), F32), V((2, 2, 8, rows, width), F32),
            V((8, rows, width), F32), V((2, 8, rows, width), F32),
            V((2, 8, rows, width), BF16), V((2, 8, rows, width), BF16),
            V((2, 8, rows, width), BF16), V((2, 8, rows, width), BF16),
            V((width, total), BF16), V((width, total), BF16),
            dma((8,)), dma((2, 8)), dma((2, 8)), dma((2, 8)), dma((2, 8)), dma((2, 16)), dma((2, 16)),
            dma((2, 4, 6)), dma((2, 4, 6)), dma((2, 4)), dma((2, 4)), dma((2, 4, 7)), dma((2, 4, 7)),
            dma((2, 2)), dma((2, 2)), dma((2,)), dma((2,)), dma((2, 8)), dma((2, 8)),
        ],
        compiler_params=pltpu.CompilerParams(collective_id=0, has_side_effects=True, **params),
    )(tokens, cotangent, w1_mask, w2_mask, bias, w1b, w2b)

    grads = jax.ShapeDtypeStruct((cap, BLK, BLK), F32)
    g1, g2, out, tg, bg = pl.pallas_call(
        block_grads,
        name="block_grads",
        out_shape=(grads, grads, small, small, jax.ShapeDtypeStruct((width,), F32)),
        in_specs=[smem, smem] + [anyw] * 4 + [vmem] * 2,
        out_specs=(anyw, anyw, vmem, vmem, vmem),
        scratch_shapes=[
            V((width, total), BF16), V((total, width), BF16), V((width, total), BF16), V((total, width), BF16),
            V((cap, BLK, BLK), F32), V((cap, BLK, BLK), F32),
            pltpu.SMEM((cap + 8,), jnp.int32), pltpu.SMEM((cap + 8,), jnp.int32),
            dma((4,)), dma((2, cap // GROUP)),
        ],
        compiler_params=pltpu.CompilerParams(**params),
    )(w1_mask, w2_mask, t, c.reshape(total, width), a, g.reshape(total, width), out, tg)
    return out, tg, g1[None, None], g2[None, None], bg


def solution(mesh):
    weights = P("row", "col", None, None, None)
    return jax.shard_map(
        local,
        mesh=mesh,
        in_specs=(P("col", "row"), P("col", "row"), P("row", "col"), weights, P("col"), P("col", "row"), weights),
        out_specs=(P("col", "row"), P("col", "row"), weights, weights, P("col")),
        check_vma=False,
    )
```

```python
import functools
import math

import jax
import jax.numpy as jnp
from jax import lax
from jax.experimental import pallas as pl
from jax.experimental.pallas import tpu as pltpu
from jax.sharding import PartitionSpec as P

MESH = pl.DeviceIdType.MESH
BLK = 128
GROUP = 8
NCH = 3
F32 = jnp.float32
BF16 = jnp.bfloat16
SLOPE = math.sqrt(2.0 / math.pi)
Z_ORDER = (4, 3, 5, 2, 6, 1, 7)
Z_WAIT = (1, 7, 2, 6, 3, 5, 4)
Y_ORDER = (2, 1, 3)


def dot_nn(a, b):
    return jnp.dot(a, b, preferred_element_type=F32)


def dot_nt(a, b):
    return lax.dot_general(a, b, (((1,), (1,)), ((), ())), preferred_element_type=F32)


def mega(
    tok, cot, m1, m2, bias, w1, w2,
    out_o, tg_o, t_o, c_o, a_o, g_o,
    t_all, c_all, a_all, g_all, w1d, w2d, wb1, wb2,
    h_send, ga_send, h_recv, ga_recv, f_send, f_recv, slope_s, bias_s,
    a_send, a_recv, own_there, own_here, b_send, b_recv, z_send, z_recv, t_turn, a_turn,
    loc, zs, zr, xs, xr, bs, br, rs_s, rs_r, fo_s, fo_r, ag_s, ag_r, la_s, la_r, lb_s, lb_r, lc_s, lc_r,
):
    width = tok.shape[1]
    cw = width // NCH
    sides = (slice(0, width // 2), slice(width // 2, width))
    row, col = lax.axis_index("row"), lax.axis_index("col")
    y, xh = row // 2, row % 2
    z, xl, k = col // 4, (col // 2) % 2, col % 2

    def col_dev(zz, xx, kk):
        return (row, zz * 4 + xx * 2 + kk)

    def row_dev(dy, dx):
        return (((y + dy) % 4) * 2 + (xh + dx) % 2, col)

    def back(d):
        return (z - d + 8) % 8

    def send(src, dst, ssem, rsem, dev):
        return pltpu.make_async_remote_copy(
            src_ref=src, dst_ref=dst, send_sem=ssem, recv_sem=rsem, device_id=dev, device_id_type=MESH
        )

    sib = col_dev(z, xl, 1 - k)
    xnb = col_dev(z, 1 - xl, k)
    partner = row_dev(0, 1)
    other = y * 2 + 1 - xh
    peers = [row_dev(d, 0) for d in Y_ORDER] + [partner]
    peers += [col_dev((z + d) % 8, xl, k) for d in range(1, 8)] + [sib, xnb]

    load1 = pltpu.make_async_copy(w1, wb1, loc.at[0])
    load2 = pltpu.make_async_copy(w2, wb2, loc.at[1])
    load1.start()
    load2.start()
    bar = pltpu.get_barrier_semaphore()
    for dev in peers:
        pl.semaphore_signal(bar, inc=1, device_id=dev, device_id_type=MESH)

    def densify(mask, blocks, dense):
        cap = blocks.shape[0]
        tr, tc = mask.shape

        def one_row(i, slot):
            for j in range(tc):
                live = mask[i, j]
                block = blocks[jnp.minimum(slot, cap - 1)]
                dense[pl.ds(pl.multiple_of(i * BLK, BLK), BLK), j * BLK:(j + 1) * BLK] = jnp.where(
                    live > 0, block, jnp.zeros_like(block)
                )
                slot = slot + live
            return slot

        lax.fori_loop(0, tr, one_row, jnp.int32(0))

    load1.wait()
    densify(m1, wb1, w1d)
    pl.semaphore_wait(bar, len(peers))

    ins, fulls = (tok, cot), (t_all, c_all)
    zc, xc, bc, own = {}, {}, {}, {}
    for a in range(2):
        src, full = ins[a], fulls[a]
        for d in Z_ORDER:
            zc[a, d] = send(src, full.at[0, z], zs.at[a, d], zr.at[a, d], col_dev((z + d) % 8, xl, k))
            zc[a, d].start()
        xc[a, 0] = send(src, full.at[2, z], xs.at[a, 0], xr.at[a, 0], xnb)
        xc[a, 0].start()
        bc[a, 0] = send(src, full.at[1, z], bs.at[a, 0], br.at[a, 0], sib)
        bc[a, 0].start()
        own[a] = pltpu.make_async_copy(src, full.at[0, z], loc.at[2 + a])
        own[a].start()
    bias_s[...] = bias[...].astype(F32).reshape(1, width)
    load2.wait()
    densify(m2, wb2, w2d)

    def forward_z(a):
        full = fulls[a]
        for d in Z_WAIT:
            zc[a, d].wait_recv()
            got = full.at[0, back(d)]
            xc[a, d] = send(got, full.at[2, back(d)], xs.at[a, d], xr.at[a, d], xnb)
            xc[a, d].start()
            bc[a, d] = send(got, full.at[1, back(d)], bs.at[a, d], br.at[a, d], sib)
            bc[a, d].start()
        own[a].wait()

    def forward_x(a):
        full = fulls[a]
        for d in (0,) + Z_WAIT:
            xc[a, d].wait_recv()
            bc[a, 8 + d] = send(
                full.at[2, back(d)], full.at[3, back(d)], bs.at[a, 8 + d], br.at[a, 8 + d], sib
            )
            bc[a, 8 + d].start()

    def arrived(a, first):
        for d in range(first, first + 8):
            bc[a, d].wait_recv()

    def cols(n):
        return pl.ds(pl.multiple_of(n * cw, cw), cw)

    def loop(body):
        lax.fori_loop(0, NCH, lambda n, c: (body(n), c)[1], 0)

    def scatter_copy(w, q, i):
        buf, got = ((h_send, h_recv), (ga_send, ga_recv))[w]
        dev = row_dev(Y_ORDER[i % 3], 0)
        share = dev[0] if i >= 3 else dev[0] + 1 - 2 * xh
        return send(buf.at[q, share], got.at[q, i], rs_s.at[w, q, i], rs_r.at[w, q, i], dev)

    def fold_copy(w, q):
        return send(f_send.at[w, q], f_recv.at[w, q], fo_s.at[w, q], fo_r.at[w, q], partner)

    def gather_copy(w, q, i):
        ref = (a_all, g_all)[w].at[q, row if i < 4 else other]
        dev = partner if i == 3 else row_dev(Y_ORDER[i % 4], 0)
        return send(ref, ref, ag_s.at[w, q, i], ag_r.at[w, q, i], dev)

    def scatter(w, quarters):
        full, buf = ((t_all, h_send), (c_all, ga_send))[w]

        def body(n):
            left = jnp.concatenate([full[q].reshape(64, width) for q in quarters], axis=0)
            part = dot_nn(left, w1d[:, cols(n)]) if w == 0 else dot_nt(left, w2d[cols(n), :])
            for at, q in enumerate(quarters):
                buf[q, :, :, cols(n)] = part[at * 64:(at + 1) * 64].reshape(8, 8, cw).astype(BF16)

        loop(body)
        for q in quarters:
            for i in range(6):
                scatter_copy(w, q, i).start()

    def fold(w, q):
        buf, got = ((h_send, h_recv), (ga_send, ga_recv))[w]
        for i in range(3):
            scatter_copy(w, q, i).wait_recv()
        total = buf[q, other].astype(F32)
        for i in range(3):
            total = total + got[q, i].astype(F32)
        f_send[w, q] = total.astype(BF16)
        fold_copy(w, q).start()

    def summed(w, q):
        buf, got = ((h_send, h_recv), (ga_send, ga_recv))[w]
        for i in range(3, 6):
            scatter_copy(w, q, i).wait_recv()
        fold_copy(w, q).wait_recv()
        total = buf[q, row].astype(F32) + f_recv[w, q].astype(F32)
        for i in range(3, 6):
            total = total + got[q, i].astype(F32)
        return total

    def spread(w, q, value):
        (a_all, g_all)[w][q, row] = value.astype(BF16)
        for i in (3, 0, 1, 2):
            gather_copy(w, q, i).start()

    def relay(w, q):
        gather_copy(w, q, 3).wait_recv()
        for i in (4, 5, 6):
            gather_copy(w, q, i).start()

    def act_part(q):
        v = summed(0, q) + bias_s[...]
        t = jnp.tanh(SLOPE * (v + 0.044715 * v * v * v))
        spread(0, q, 0.5 * v * (1.0 + t))
        slope_s[q] = 0.5 * (1.0 + t) + 0.5 * v * (1.0 - t * t) * SLOPE * (
            1.0 + 3.0 * 0.044715 * v * v
        )

    def gh_part(q):
        spread(1, q, summed(1, q) * slope_s[q])

    stores = []

    def store(src, dst):
        stores.append(pltpu.make_async_copy(src, dst, loc.at[4 + len(stores)]))
        stores[-1].start()

    def turn(src, dst):
        def body(n):
            dst[cols(n), :] = src[:, :, :, cols(n)].reshape(256, cw).astype(F32).T.astype(BF16)

        loop(body)

    def copy_a(w, part):
        return send(a_send.at[w, part], a_recv.at[w, part], la_s.at[w, part], la_r.at[w, part], sib)

    def copy_b(w, h):
        return send(b_send.at[w, h], b_recv.at[w, h], lb_s.at[w, h], lb_r.at[w, h], xnb)

    def copy_c(w, h, d):
        zz = (z + d) % 8
        return send(
            z_send.at[w, h, zz], z_recv.at[w, h, d], lc_s.at[w, h, d], lc_r.at[w, h, d], col_dev(zz, xl, k)
        )

    def project(w, q, put):
        full = (a_all, g_all)[w]
        for i in (0, 1, 2, 4, 5, 6):
            gather_copy(w, q, i).wait_recv()

        def body(n):
            left = full[q].reshape(64, width)
            part = dot_nn(left, w2d[:, cols(n)]) if w == 0 else dot_nt(left, w1d[cols(n), :])
            put(n, part.reshape(8, 8, cw))

        loop(body)

    def to_sibling(w, part, q):
        def put(n, value):
            a_send[w, part, :, :, cols(n)] = value

        project(w, q, put)
        copy_a(w, part).start()

    def far_half(w):
        to_sibling(w, 0, 3)

        def put(n, value):
            own_there[:, :, cols(n)] = value

        project(w, 2, put)
        copy_a(w, 0).wait_recv()
        for h, side in enumerate(sides):
            b_send[w, h] = (own_there[:, :, side] + a_recv[w, 0, :, :, side]).astype(BF16)
            copy_b(w, h).start()

    def near_half(w):
        to_sibling(w, 1, 1)

        def put(n, value):
            own_here[w, :, :, cols(n)] = value

        project(w, 0, put)

    def over_z(w):
        copy_a(w, 1).wait_recv()
        for h, side in enumerate(sides):
            copy_b(w, h).wait_recv()
            total = own_here[w, :, :, side] + a_recv[w, 1, :, :, side] + b_recv[w, h].astype(F32)
            own_here[w, :, :, side] = total
            z_send[w, h] = total.astype(BF16)
            for d in Z_ORDER:
                copy_c(w, h, d).start()

    def last(w):
        for h, side in enumerate(sides):
            total = own_here[w, z, :, side]
            for d in Z_WAIT:
                copy_c(w, h, d).wait_recv()
            for d in range(1, 8):
                total = total + z_recv[w, h, d].astype(F32)
            (out_o, tg_o)[w][:, side] = total.astype(BF16)

    forward_z(0)
    scatter(0, (0,))
    forward_z(1)
    forward_x(0)
    arrived(0, 0)
    scatter(0, (1,))
    arrived(0, 8)
    scatter(0, (2, 3))
    forward_x(1)
    fold(0, 0)
    fold(0, 1)
    arrived(1, 0)
    scatter(1, (0, 1))
    fold(0, 2)
    fold(0, 3)
    arrived(1, 8)
    scatter(1, (2, 3))
    for q in (3, 2, 1, 0):
        act_part(q)
    turn(t_all, t_turn)
    store(t_turn, t_o)
    store(c_all, c_o)
    for q in (3, 2):
        relay(0, q)
    for q in (3, 2):
        fold(1, q)
    for q in (1, 0):
        relay(0, q)
    for q in (1, 0):
        fold(1, q)
    for q in (3, 2):
        gh_part(q)
    for q in (1, 0):
        gh_part(q)
    for q in (3, 2, 1, 0):
        relay(1, q)
    far_half(0)
    near_half(0)
    turn(a_all, a_turn)
    store(a_turn, a_o)
    far_half(1)
    over_z(0)
    near_half(1)
    store(g_all, g_o)
    over_z(1)
    last(0)
    last(1)

    for table in (zc, xc, bc):
        for copy in table.values():
            copy.wait_send()
    for w in range(2):
        for q in range(4):
            for i in range(6):
                scatter_copy(w, q, i).wait_send()
            fold_copy(w, q).wait_send()
            for i in range(7):
                gather_copy(w, q, i).wait_send()
        copy_a(w, 0).wait_send()
        copy_a(w, 1).wait_send()
        for h in range(2):
            copy_b(w, h).wait_send()
            for d in range(1, 8):
                copy_c(w, h, d).wait_send()
    for s in stores:
        s.wait()


def block_grads(
    m1, m2, t_h, c_h, a_h, g_h, out_i, tg_i, g1_o, g2_o, out_o, tg_o, bg_o,
    t, c, a, g, b1, b2, i1, i2, sems, puts,
):
    groups = b1.shape[0] // GROUP
    loads = [
        pltpu.make_async_copy(src, dst, sems.at[i])
        for i, (src, dst) in enumerate(((g_h, g), (t_h, t), (a_h, a), (c_h, c)))
    ]
    for load in loads:
        load.start()
    out_o[...] = out_i[...]
    tg_o[...] = tg_i[...]
    counts = []
    for mask, table in ((m1, i1), (m2, i2)):
        tr, tc = mask.shape

        def one_row(i, slot):
            for j in range(tc):
                table[slot] = i * tc + j
                slot = slot + mask[i, j]
            return slot

        counts.append(lax.fori_loop(0, tr, one_row, jnp.int32(0)))

    def tall(ref, i):
        return ref[pl.ds(pl.multiple_of(i * BLK, BLK), BLK), :]

    def wide(ref, i):
        return ref[:, pl.ds(pl.multiple_of(i * BLK, BLK), BLK)]

    def put(which, at):
        src, dst = ((b1, g1_o), (b2, g2_o))[which]
        part = pl.ds(at * GROUP, GROUP)
        return pltpu.make_async_copy(src.at[part], dst.at[part], puts.at[which, at])

    for which, (left, right, mask, table, dest) in enumerate(((t, g, m1, i1, b1), (a, c, m2, i2, b2))):
        tc = mask.shape[1]
        loads[2 * which].wait()
        loads[2 * which + 1].wait()

        def one_group(at, carry):
            for u in range(GROUP):
                slot = at * GROUP + u
                live = slot < counts[which]
                place = jnp.where(live, table[slot], 0)
                grad = dot_nn(tall(left, place // tc), wide(right, place % tc))
                dest[slot] = jnp.where(live, grad, 0.0)
            put(which, at).start()
            return carry

        lax.fori_loop(0, groups, one_group, 0)
    bg_o[...] = jnp.sum(g[...].astype(F32), axis=0)
    for which in range(2):
        lax.fori_loop(0, groups, lambda at, x: (put(which, at).wait(), x)[1], 0)


def local(tokens, cotangent, w1_mask, w1_blocks, bias, w2_mask, w2_blocks):
    rows, width = tokens.shape
    total = 256
    cap = w1_blocks.shape[2]
    w1b = w1_blocks.reshape(w1_blocks.shape[2:])
    w2b = w2_blocks.reshape(w2_blocks.shape[2:])
    vmem = pl.BlockSpec(memory_space=pltpu.VMEM)
    smem = pl.BlockSpec(memory_space=pltpu.SMEM)
    anyw = pl.BlockSpec(memory_space=pl.ANY)
    small = jax.ShapeDtypeStruct((rows, width), BF16)
    turned = jax.ShapeDtypeStruct((width, total), BF16)
    quarters = (4, 8, rows, width)
    full = jax.ShapeDtypeStruct(quarters, BF16)
    dma = pltpu.SemaphoreType.DMA
    V = pltpu.VMEM
    params = dict(vmem_limit_bytes=67043328)
    out, tg, t, c, a, g = pl.pallas_call(
        mega,
        name="mega",
        out_shape=(small, small, turned, full, turned, full),
        in_specs=[vmem, vmem, smem, smem, vmem, anyw, anyw],
        out_specs=(vmem, vmem, anyw, anyw, anyw, anyw),
        scratch_shapes=[
            V(quarters, BF16), V(quarters, BF16), V(quarters, BF16), V(quarters, BF16),
            V((width, width), BF16), V((width, width), BF16),
            V((cap, BLK, BLK), BF16), V((cap, BLK, BLK), BF16),
            V(quarters, BF16), V(quarters, BF16),
            V((4, 6, rows, width), BF16), V((4, 6, rows, width), BF16),
            V((2, 4, rows, width), BF16), V((2, 4, rows, width), BF16),
            V((4, rows, width), F32), V((1, width), F32),
            V((2, 2, 8, rows, width), F32), V((2, 2, 8, rows, width), F32),
            V((8, rows, width), F32), V((2, 8, rows, width), F32),
            V((2, 2, 8, rows, width // 2), BF16), V((2, 2, 8, rows, width // 2), BF16),
            V((2, 2, 8, rows, width // 2), BF16), V((2, 2, 8, rows, width // 2), BF16),
            V((width, total), BF16), V((width, total), BF16),
            dma((8,)), dma((2, 8)), dma((2, 8)), dma((2, 8)), dma((2, 8)), dma((2, 16)), dma((2, 16)),
            dma((2, 4, 6)), dma((2, 4, 6)), dma((2, 4)), dma((2, 4)), dma((2, 4, 7)), dma((2, 4, 7)),
            dma((2, 2)), dma((2, 2)), dma((2, 2)), dma((2, 2)), dma((2, 2, 8)), dma((2, 2, 8)),
        ],
        compiler_params=pltpu.CompilerParams(collective_id=0, has_side_effects=True, **params),
    )(tokens, cotangent, w1_mask, w2_mask, bias, w1b, w2b)

    grads = jax.ShapeDtypeStruct((cap, BLK, BLK), F32)
    g1, g2, out, tg, bg = pl.pallas_call(
        block_grads,
        name="block_grads",
        out_shape=(grads, grads, small, small, jax.ShapeDtypeStruct((width,), F32)),
        in_specs=[smem, smem] + [anyw] * 4 + [vmem] * 2,
        out_specs=(anyw, anyw, vmem, vmem, vmem),
        scratch_shapes=[
            V((width, total), BF16), V((total, width), BF16), V((width, total), BF16), V((total, width), BF16),
            V((cap, BLK, BLK), F32), V((cap, BLK, BLK), F32),
            pltpu.SMEM((cap + 8,), jnp.int32), pltpu.SMEM((cap + 8,), jnp.int32),
            dma((4,)), dma((2, cap // GROUP)),
        ],
        compiler_params=pltpu.CompilerParams(**params),
    )(w1_mask, w2_mask, t, c.reshape(total, width), a, g.reshape(total, width), out, tg)
    return out, tg, g1[None, None], g2[None, None], bg


def solution(mesh):
    weights = P("row", "col", None, None, None)
    return jax.shard_map(
        local,
        mesh=mesh,
        in_specs=(P("col", "row"), P("col", "row"), P("row", "col"), weights, P("col"), P("col", "row"), weights),
        out_specs=(P("col", "row"), P("col", "row"), weights, weights, P("col")),
        check_vma=False,
    )
```

```python
import functools
import math

import jax
import jax.numpy as jnp
from jax import lax
from jax.experimental import pallas as pl
from jax.experimental.pallas import tpu as pltpu
from jax.sharding import PartitionSpec as P

MESH = pl.DeviceIdType.MESH
BLK = 128
GROUP = 16
NCH = 3
F32 = jnp.float32
BF16 = jnp.bfloat16
SLOPE = math.sqrt(2.0 / math.pi)
Z_ORDER = (4, 3, 5, 2, 6, 1, 7)
Z_WAIT = (1, 7, 2, 6, 3, 5, 4)
Y_ORDER = (2, 1, 3)


def dot_nn(a, b):
    return jnp.dot(a, b, preferred_element_type=F32)


def dot_nt(a, b):
    return lax.dot_general(a, b, (((1,), (1,)), ((), ())), preferred_element_type=F32)


def mega(
    tok, cot, m1, m2, bias, w1, w2,
    out_o, tg_o, t_o, c_o, a_o, g_o,
    t_all, c_all, a_all, g_all, w1d, w2d, wb1, wb2,
    h_send, ga_send, h_recv, ga_recv, f_send, f_recv, slope_s, bias_s,
    a_send, a_recv, own_there, own_here, b_send, b_recv, z_send, z_recv, t_turn, a_turn,
    loc, zs, zr, xs, xr, bs, br, rs_s, rs_r, fo_s, fo_r, ag_s, ag_r, la_s, la_r, lb_s, lb_r, lc_s, lc_r,
):
    width = tok.shape[1]
    cw = width // NCH
    sides = (slice(0, width // 2), slice(width // 2, width))
    row, col = lax.axis_index("row"), lax.axis_index("col")
    y, xh = row // 2, row % 2
    z, xl, k = col // 4, (col // 2) % 2, col % 2

    def col_dev(zz, xx, kk):
        return (row, zz * 4 + xx * 2 + kk)

    def row_dev(dy, dx):
        return (((y + dy) % 4) * 2 + (xh + dx) % 2, col)

    def back(d):
        return (z - d + 8) % 8

    def send(src, dst, ssem, rsem, dev):
        return pltpu.make_async_remote_copy(
            src_ref=src, dst_ref=dst, send_sem=ssem, recv_sem=rsem, device_id=dev, device_id_type=MESH
        )

    sib = col_dev(z, xl, 1 - k)
    xnb = col_dev(z, 1 - xl, k)
    partner = row_dev(0, 1)
    other = y * 2 + 1 - xh
    peers = [row_dev(d, 0) for d in Y_ORDER] + [partner]
    peers += [col_dev((z + d) % 8, xl, k) for d in range(1, 8)] + [sib, xnb]

    load1 = pltpu.make_async_copy(w1, wb1, loc.at[0])
    load2 = pltpu.make_async_copy(w2, wb2, loc.at[1])
    load1.start()
    load2.start()
    bar = pltpu.get_barrier_semaphore()
    for dev in peers:
        pl.semaphore_signal(bar, inc=1, device_id=dev, device_id_type=MESH)

    def densify(mask, blocks, dense):
        cap = blocks.shape[0]
        tr, tc = mask.shape

        def one_row(i, slot):
            for j in range(tc):
                live = mask[i, j]
                block = blocks[jnp.minimum(slot, cap - 1)]
                dense[pl.ds(pl.multiple_of(i * BLK, BLK), BLK), j * BLK:(j + 1) * BLK] = jnp.where(
                    live > 0, block, jnp.zeros_like(block)
                )
                slot = slot + live
            return slot

        lax.fori_loop(0, tr, one_row, jnp.int32(0))

    load1.wait()
    densify(m1, wb1, w1d)
    pl.semaphore_wait(bar, len(peers))

    ins, fulls = (tok, cot), (t_all, c_all)
    zc, xc, bc, own = {}, {}, {}, {}
    for a in range(2):
        src, full = ins[a], fulls[a]
        for d in Z_ORDER:
            zc[a, d] = send(src, full.at[0, z], zs.at[a, d], zr.at[a, d], col_dev((z + d) % 8, xl, k))
            zc[a, d].start()
        xc[a, 0] = send(src, full.at[2, z], xs.at[a, 0], xr.at[a, 0], xnb)
        xc[a, 0].start()
        bc[a, 0] = send(src, full.at[1, z], bs.at[a, 0], br.at[a, 0], sib)
        bc[a, 0].start()
        own[a] = pltpu.make_async_copy(src, full.at[0, z], loc.at[2 + a])
        own[a].start()
    bias_s[...] = bias[...].astype(F32).reshape(1, width)
    load2.wait()
    densify(m2, wb2, w2d)

    def forward_z(a):
        full = fulls[a]
        for d in Z_WAIT:
            zc[a, d].wait_recv()
            got = full.at[0, back(d)]
            xc[a, d] = send(got, full.at[2, back(d)], xs.at[a, d], xr.at[a, d], xnb)
            xc[a, d].start()
            bc[a, d] = send(got, full.at[1, back(d)], bs.at[a, d], br.at[a, d], sib)
            bc[a, d].start()
        own[a].wait()

    def forward_x(a):
        full = fulls[a]
        for d in (0,) + Z_WAIT:
            xc[a, d].wait_recv()
            bc[a, 8 + d] = send(
                full.at[2, back(d)], full.at[3, back(d)], bs.at[a, 8 + d], br.at[a, 8 + d], sib
            )
            bc[a, 8 + d].start()

    def arrived(a, first):
        for d in range(first, first + 8):
            bc[a, d].wait_recv()

    def cols(n):
        return pl.ds(pl.multiple_of(n * cw, cw), cw)

    def loop(body):
        lax.fori_loop(0, NCH, lambda n, c: (body(n), c)[1], 0)

    def scatter_copy(w, q, i):
        buf, got = ((h_send, h_recv), (ga_send, ga_recv))[w]
        dev = row_dev(Y_ORDER[i % 3], 0)
        share = dev[0] if i >= 3 else dev[0] + 1 - 2 * xh
        return send(buf.at[q, share], got.at[q, i], rs_s.at[w, q, i], rs_r.at[w, q, i], dev)

    def fold_copy(w, q):
        return send(f_send.at[w, q], f_recv.at[w, q], fo_s.at[w, q], fo_r.at[w, q], partner)

    def gather_copy(w, q, i):
        ref = (a_all, g_all)[w].at[q, row if i < 4 else other]
        dev = partner if i == 3 else row_dev(Y_ORDER[i % 4], 0)
        return send(ref, ref, ag_s.at[w, q, i], ag_r.at[w, q, i], dev)

    def scatter(w, quarters):
        full, buf = ((t_all, h_send), (c_all, ga_send))[w]

        def body(n):
            left = jnp.concatenate([full[q].reshape(64, width) for q in quarters], axis=0)
            part = dot_nn(left, w1d[:, cols(n)]) if w == 0 else dot_nt(left, w2d[cols(n), :])
            for at, q in enumerate(quarters):
                buf[q, :, :, cols(n)] = part[at * 64:(at + 1) * 64].reshape(8, 8, cw).astype(BF16)

        loop(body)
        for q in quarters:
            for i in range(6):
                scatter_copy(w, q, i).start()

    def fold(w, q):
        buf, got = ((h_send, h_recv), (ga_send, ga_recv))[w]
        for i in range(3):
            scatter_copy(w, q, i).wait_recv()
        total = buf[q, other].astype(F32)
        for i in range(3):
            total = total + got[q, i].astype(F32)
        f_send[w, q] = total.astype(BF16)
        fold_copy(w, q).start()

    def summed(w, q):
        buf, got = ((h_send, h_recv), (ga_send, ga_recv))[w]
        for i in range(3, 6):
            scatter_copy(w, q, i).wait_recv()
        fold_copy(w, q).wait_recv()
        total = buf[q, row].astype(F32) + f_recv[w, q].astype(F32)
        for i in range(3, 6):
            total = total + got[q, i].astype(F32)
        return total

    def spread(w, q, value):
        (a_all, g_all)[w][q, row] = value.astype(BF16)
        for i in (3, 0, 1, 2):
            gather_copy(w, q, i).start()

    def relay(w, q):
        gather_copy(w, q, 3).wait_recv()
        for i in (4, 5, 6):
            gather_copy(w, q, i).start()

    def act_part(q):
        v = summed(0, q) + bias_s[...]
        t = jnp.tanh(SLOPE * (v + 0.044715 * v * v * v))
        spread(0, q, 0.5 * v * (1.0 + t))
        slope_s[q] = 0.5 * (1.0 + t) + 0.5 * v * (1.0 - t * t) * SLOPE * (
            1.0 + 3.0 * 0.044715 * v * v
        )

    def gh_part(q):
        spread(1, q, summed(1, q) * slope_s[q])

    stores = []

    def store(src, dst):
        stores.append(pltpu.make_async_copy(src, dst, loc.at[4 + len(stores)]))
        stores[-1].start()

    def turn(src, dst):
        def body(n):
            dst[cols(n), :] = src[:, :, :, cols(n)].reshape(256, cw).astype(F32).T.astype(BF16)

        loop(body)

    def copy_a(w, part):
        return send(a_send.at[w, part], a_recv.at[w, part], la_s.at[w, part], la_r.at[w, part], sib)

    def copy_b(w, h):
        return send(b_send.at[w, h], b_recv.at[w, h], lb_s.at[w, h], lb_r.at[w, h], xnb)

    def copy_c(w, h, d):
        zz = (z + d) % 8
        return send(
            z_send.at[w, h, zz], z_recv.at[w, h, d], lc_s.at[w, h, d], lc_r.at[w, h, d], col_dev(zz, xl, k)
        )

    def project(w, q, put):
        full = (a_all, g_all)[w]
        for i in (0, 1, 2, 4, 5, 6):
            gather_copy(w, q, i).wait_recv()

        def body(n):
            left = full[q].reshape(64, width)
            part = dot_nn(left, w2d[:, cols(n)]) if w == 0 else dot_nt(left, w1d[cols(n), :])
            put(n, part.reshape(8, 8, cw))

        loop(body)

    def to_sibling(w, part, q):
        def put(n, value):
            a_send[w, part, :, :, cols(n)] = value

        project(w, q, put)
        copy_a(w, part).start()

    def far_half(w):
        to_sibling(w, 0, 3)

        def put(n, value):
            own_there[:, :, cols(n)] = value

        project(w, 2, put)
        copy_a(w, 0).wait_recv()
        for h, side in enumerate(sides):
            b_send[w, h] = (own_there[:, :, side] + a_recv[w, 0, :, :, side]).astype(BF16)
            copy_b(w, h).start()

    def near_half(w):
        to_sibling(w, 1, 1)

        def put(n, value):
            own_here[w, :, :, cols(n)] = value

        project(w, 0, put)

    def over_z(w):
        copy_a(w, 1).wait_recv()
        for h, side in enumerate(sides):
            copy_b(w, h).wait_recv()
            total = own_here[w, :, :, side] + a_recv[w, 1, :, :, side] + b_recv[w, h].astype(F32)
            own_here[w, :, :, side] = total
            z_send[w, h] = total.astype(BF16)
            for d in Z_ORDER:
                copy_c(w, h, d).start()

    def last(w):
        for h, side in enumerate(sides):
            total = own_here[w, z, :, side]
            for d in Z_WAIT:
                copy_c(w, h, d).wait_recv()
            for d in range(1, 8):
                total = total + z_recv[w, h, d].astype(F32)
            (out_o, tg_o)[w][:, side] = total.astype(BF16)

    forward_z(0)
    scatter(0, (0,))
    forward_z(1)
    forward_x(0)
    arrived(0, 0)
    scatter(0, (1,))
    arrived(0, 8)
    scatter(0, (2, 3))
    forward_x(1)
    fold(0, 0)
    fold(0, 1)
    arrived(1, 0)
    scatter(1, (0, 1))
    fold(0, 2)
    fold(0, 3)
    arrived(1, 8)
    scatter(1, (2, 3))
    for q in (3, 2, 1, 0):
        act_part(q)
    turn(t_all, t_turn)
    store(t_turn, t_o)
    store(c_all, c_o)
    for q in (3, 2):
        relay(0, q)
    for q in (3, 2):
        fold(1, q)
    for q in (1, 0):
        relay(0, q)
    for q in (1, 0):
        fold(1, q)
    for q in (3, 2):
        gh_part(q)
    for q in (1, 0):
        gh_part(q)
    for q in (3, 2, 1, 0):
        relay(1, q)
    far_half(0)
    near_half(0)
    turn(a_all, a_turn)
    store(a_turn, a_o)
    far_half(1)
    over_z(0)
    near_half(1)
    store(g_all, g_o)
    over_z(1)
    last(0)
    last(1)

    for table in (zc, xc, bc):
        for copy in table.values():
            copy.wait_send()
    for w in range(2):
        for q in range(4):
            for i in range(6):
                scatter_copy(w, q, i).wait_send()
            fold_copy(w, q).wait_send()
            for i in range(7):
                gather_copy(w, q, i).wait_send()
        copy_a(w, 0).wait_send()
        copy_a(w, 1).wait_send()
        for h in range(2):
            copy_b(w, h).wait_send()
            for d in range(1, 8):
                copy_c(w, h, d).wait_send()
    for s in stores:
        s.wait()


def block_grads(
    m1, m2, t_h, c_h, a_h, g_h, out_i, tg_i, g1_o, g2_o, out_o, tg_o, bg_o,
    t, c, a, g, b1, b2, i1, i2, sems, puts,
):
    groups = b1.shape[0] // GROUP
    loads = [
        pltpu.make_async_copy(src, dst, sems.at[i])
        for i, (src, dst) in enumerate(((g_h, g), (t_h, t), (a_h, a), (c_h, c)))
    ]
    for load in loads:
        load.start()
    out_o[...] = out_i[...]
    tg_o[...] = tg_i[...]
    counts = []
    for mask, table in ((m1, i1), (m2, i2)):
        tr, tc = mask.shape

        def one_row(i, slot):
            for j in range(tc):
                table[slot] = i * tc + j
                slot = slot + mask[i, j]
            return slot

        counts.append(lax.fori_loop(0, tr, one_row, jnp.int32(0)))

    def tall(ref, i):
        return ref[pl.ds(pl.multiple_of(i * BLK, BLK), BLK), :]

    def wide(ref, i):
        return ref[:, pl.ds(pl.multiple_of(i * BLK, BLK), BLK)]

    def put(which, at):
        src, dst = ((b1, g1_o), (b2, g2_o))[which]
        part = pl.ds(at * GROUP, GROUP)
        return pltpu.make_async_copy(src.at[part], dst.at[part], puts.at[which, at])

    for which, (left, right, mask, table, dest) in enumerate(((t, g, m1, i1, b1), (a, c, m2, i2, b2))):
        tc = mask.shape[1]
        loads[2 * which].wait()
        loads[2 * which + 1].wait()

        def one_group(at, carry):
            for u in range(GROUP):
                slot = at * GROUP + u
                live = slot < counts[which]
                place = jnp.where(live, table[slot], 0)
                grad = dot_nn(tall(left, place // tc), wide(right, place % tc))
                dest[slot] = jnp.where(live, grad, 0.0)
            put(which, at).start()
            return carry

        lax.fori_loop(0, groups, one_group, 0)
    bg_o[...] = jnp.sum(g[...].astype(F32), axis=0)
    for which in range(2):
        lax.fori_loop(0, groups, lambda at, x: (put(which, at).wait(), x)[1], 0)


def local(tokens, cotangent, w1_mask, w1_blocks, bias, w2_mask, w2_blocks):
    rows, width = tokens.shape
    total = 256
    cap = w1_blocks.shape[2]
    w1b = w1_blocks.reshape(w1_blocks.shape[2:])
    w2b = w2_blocks.reshape(w2_blocks.shape[2:])
    vmem = pl.BlockSpec(memory_space=pltpu.VMEM)
    smem = pl.BlockSpec(memory_space=pltpu.SMEM)
    anyw = pl.BlockSpec(memory_space=pl.ANY)
    small = jax.ShapeDtypeStruct((rows, width), BF16)
    turned = jax.ShapeDtypeStruct((width, total), BF16)
    quarters = (4, 8, rows, width)
    full = jax.ShapeDtypeStruct(quarters, BF16)
    dma = pltpu.SemaphoreType.DMA
    V = pltpu.VMEM
    params = dict(vmem_limit_bytes=67043328)
    out, tg, t, c, a, g = pl.pallas_call(
        mega,
        name="mega",
        out_shape=(small, small, turned, full, turned, full),
        in_specs=[vmem, vmem, smem, smem, vmem, anyw, anyw],
        out_specs=(vmem, vmem, anyw, anyw, anyw, anyw),
        scratch_shapes=[
            V(quarters, BF16), V(quarters, BF16), V(quarters, BF16), V(quarters, BF16),
            V((width, width), BF16), V((width, width), BF16),
            V((cap, BLK, BLK), BF16), V((cap, BLK, BLK), BF16),
            V(quarters, BF16), V(quarters, BF16),
            V((4, 6, rows, width), BF16), V((4, 6, rows, width), BF16),
            V((2, 4, rows, width), BF16), V((2, 4, rows, width), BF16),
            V((4, rows, width), F32), V((1, width), F32),
            V((2, 2, 8, rows, width), F32), V((2, 2, 8, rows, width), F32),
            V((8, rows, width), F32), V((2, 8, rows, width), F32),
            V((2, 2, 8, rows, width // 2), BF16), V((2, 2, 8, rows, width // 2), BF16),
            V((2, 2, 8, rows, width // 2), BF16), V((2, 2, 8, rows, width // 2), BF16),
            V((width, total), BF16), V((width, total), BF16),
            dma((8,)), dma((2, 8)), dma((2, 8)), dma((2, 8)), dma((2, 8)), dma((2, 16)), dma((2, 16)),
            dma((2, 4, 6)), dma((2, 4, 6)), dma((2, 4)), dma((2, 4)), dma((2, 4, 7)), dma((2, 4, 7)),
            dma((2, 2)), dma((2, 2)), dma((2, 2)), dma((2, 2)), dma((2, 2, 8)), dma((2, 2, 8)),
        ],
        compiler_params=pltpu.CompilerParams(collective_id=0, has_side_effects=True, **params),
    )(tokens, cotangent, w1_mask, w2_mask, bias, w1b, w2b)

    grads = jax.ShapeDtypeStruct((cap, BLK, BLK), F32)
    g1, g2, out, tg, bg = pl.pallas_call(
        block_grads,
        name="block_grads",
        out_shape=(grads, grads, small, small, jax.ShapeDtypeStruct((width,), F32)),
        in_specs=[smem, smem] + [anyw] * 4 + [vmem] * 2,
        out_specs=(anyw, anyw, vmem, vmem, vmem),
        scratch_shapes=[
            V((width, total), BF16), V((total, width), BF16), V((width, total), BF16), V((total, width), BF16),
            V((cap, BLK, BLK), F32), V((cap, BLK, BLK), F32),
            pltpu.SMEM((cap + 8,), jnp.int32), pltpu.SMEM((cap + 8,), jnp.int32),
            dma((4,)), dma((2, cap // GROUP)),
        ],
        compiler_params=pltpu.CompilerParams(**params),
    )(w1_mask, w2_mask, t, c.reshape(total, width), a, g.reshape(total, width), out, tg)
    return out, tg, g1[None, None], g2[None, None], bg


def solution(mesh):
    weights = P("row", "col", None, None, None)
    return jax.shard_map(
        local,
        mesh=mesh,
        in_specs=(P("col", "row"), P("col", "row"), P("row", "col"), weights, P("col"), P("col", "row"), weights),
        out_specs=(P("col", "row"), P("col", "row"), weights, weights, P("col")),
        check_vma=False,
    )
```
